256 devices in a mesh: feat: 8 (over y, z_lo), rows: 32 (over x, z_hi, core).
Axes of the slice: x: 4, y: 4, z: 8 (z_hi: 4, z_lo: 2; z = z_hi * 2 + z_lo), core: 2. Of those that a mesh axis runs over, the one named last changes fastest.
Arguments:
- x_vals: bfloat16 [64, 8, 8, 512, 128], P('rows', 'feat'), may hold values from -6 to 6
- x_blocks: int32 [64, 8, 8], P('rows', 'feat'), may hold values from 0 to 195
- y_vals: bfloat16 [32, 8, 8, 512, 128], P('rows', 'feat'), may hold values from -6 to 6
- y_blocks: int32 [32, 8, 8], P('rows', 'feat'), may hold values from 0 to 97
- user_weights: bfloat16 [256, 200704], P('rows', 'feat'), may hold values from -0.0625 to 0.0625
- item_weights: bfloat16 [256, 100352], P('rows', 'feat'), may hold values from -0.0625 to 0.0625
- observed: int32 [64, 32], P('rows'), may hold values 0 or 1
- ratings: bfloat16 [32768, 8, 2048], P('rows', 'feat'), may hold values from -6 to 6
Outputs:
- grad_user: float32 [256, 200704], P('rows', 'feat')
- grad_item: float32 [256, 100352], P('rows', 'feat')
The draws below stay inside these ranges and needn't reach their ends.
Inputs may be any that keep to these rules, and one draw needn't show every extreme that they name: `x_blocks`: feature block numbers within one shard. `y_blocks`: feature block numbers within one shard.
All inputs are finite; a program needn't handle non-finite values. No bound on the sum of `observed` on one device may be relied on, other than what follows from the above.
Results may differ from the reference program's by a relative error of at most 0.008.
Values may be sent and summed in bfloat16 or wider, within the bound.
A program may use at most 64 MiB of HBM per device.

```python
import math
import jax
import jax.numpy as jnp
import numpy as np
from jax import lax

TILE = 512
FBW = 128
RANK = 256
FU = 200704
FI = 100352
KBF = 8
KBI = 8
NUB = 64
NIB = 32
USERS = 32768
ITEMS = 16384
IS = 64
FBS_U = 196
FBS_I = 98
N_FEAT = 8
N_ROWS = 32


def with_ends(result, rng, low, top_value):
    spot = [jax.random.randint(jax.random.fold_in(rng, axis), (), 0, length) for axis, length in enumerate(result.shape)]
    widest = result.shape.index(max(result.shape))
    neighbour = spot[:widest] + [(spot[widest] + 1) % result.shape[widest]] + spot[widest + 1:]
    return result.at[tuple(spot)].set(low).at[tuple(neighbour)].set(top_value)


def levels(rng, extent, split, smallest, largest):
    def one(position, shards_of):
        heights = jax.random.uniform(jax.random.fold_in(jax.random.fold_in(rng, 6), position), (shards_of,), jnp.float32, smallest / len(split), largest / len(split))
        return jnp.repeat(jnp.exp(heights), extent[position] // shards_of).reshape((-1,) + (1,) * (len(extent) - position - 1))

    loudness = one(*split[0])
    for cut in split[1:]:
        loudness = loudness * one(*cut)
    return loudness


def rank_table(amount, slope):
    portions = [(1 << 20) // math.isqrt(grade ** slope) + 1 for grade in range(1, amount + 1)]
    scale = 1 + sum(portions) // (1 << 30)
    return np.cumsum(np.array([max(1, weight // scale) for weight in portions]))


def ranked_ids(rng, shape, number_of, slope):
    listing = rank_table(number_of, slope)
    lot = jax.random.randint(jax.random.fold_in(rng, 1), shape, 0, int(listing[number_of - 1]))
    standing = jnp.searchsorted(jnp.asarray(listing, jnp.int32), lot, side="right")
    return jax.random.permutation(jax.random.fold_in(rng, 2), number_of)[standing].astype(jnp.int32)


def normal_values(rng, shape, scale, reach, pieces=(), kind=jnp.bfloat16):
    array = scale * jax.random.normal(rng, shape, jnp.float32)
    if pieces:
        array = array * levels(rng, shape, pieces, -0.22, 0.18)
    return jnp.clip(array, -reach, reach).astype(kind)


def setup_inputs(seed: int = 0) -> dict:
    arg_keys = jax.random.split(jax.random.key(seed), 9)
    return {
        "x_vals": normal_values(arg_keys[0], (NUB, N_FEAT, KBF, TILE, FBW), 1.0, 6.0, ((0, 32), (1, 8))),
        "x_blocks": with_ends(ranked_ids(arg_keys[1], (NUB, N_FEAT, KBF), FBS_U, 2), jax.random.fold_in(arg_keys[1], 3), 0, FBS_U - 1).astype(jnp.int32),
        "y_vals": normal_values(arg_keys[2], (NIB, N_FEAT, KBI, TILE, FBW), 1.0, 6.0, ((0, 32), (1, 8))),
        "y_blocks": with_ends(ranked_ids(arg_keys[3], (NIB, N_FEAT, KBI), FBS_I, 2), jax.random.fold_in(arg_keys[3], 3), 0, FBS_I - 1).astype(jnp.int32),
        "user_weights": normal_values(arg_keys[4], (RANK, FU), (KBF * N_FEAT * FBW) ** -0.5, 0.0625, ((0, 32), (1, 8))),
        "item_weights": normal_values(arg_keys[5], (RANK, FI), (KBI * N_FEAT * FBW) ** -0.5, 0.0625, ((0, 32), (1, 8))),
        "observed": with_ends((jax.random.randint(arg_keys[6], (NUB, NIB), 0, 2) < 1).astype(jnp.int32), jax.random.fold_in(arg_keys[6], 1), 0, 1),
        "ratings": normal_values(arg_keys[7], (USERS, N_FEAT, ITEMS // N_FEAT), 1.0, 6.0, ((0, 32), (1, 8))),
    }


def project(values, indices, weights_t, shard_blocks):
    blocks_table = weights_t.reshape(RANK, N_FEAT, shard_blocks, FBW)
    feat_index = jnp.arange(N_FEAT, dtype=jnp.int32)[:, None]

    def project_block(pair):
        block_values, block_indices = pair
        chosen = blocks_table[:, feat_index, block_indices.astype(jnp.int32)]
        return jnp.einsum('fktc,rfkc->tr', block_values.astype(jnp.float32), chosen.astype(jnp.float32))
    summed = lax.map(project_block, (values, indices))
    return summed.reshape(-1, RANK).astype(jnp.bfloat16)

def block_grads(values, indices, grads, shard_blocks):
    feat_index = jnp.arange(N_FEAT, dtype=jnp.int32)[:, None]
    totals = jnp.zeros((RANK, N_FEAT, shard_blocks, FBW), jnp.float32)

    def add_block(current, triple):
        block_values, block_indices, block_grads_now = triple
        contrib = jnp.einsum('tr,fktc->rfkc', block_grads_now.astype(jnp.float32), block_values.astype(jnp.float32))
        return (current.at[:, feat_index, block_indices.astype(jnp.int32)].add(contrib), None)
    totals, unused = lax.scan(add_block, totals, (values, indices, grads.reshape(-1, TILE, RANK)))
    return totals.reshape(RANK, -1)

def reference(x_vals, x_blocks, y_vals, y_blocks, user_weights, item_weights, observed, ratings):
    rank_scale = 1.0 / math.sqrt(RANK)
    grad_scale = 1.0 / (TILE * math.sqrt(RANK))
    user_proj = project(x_vals, x_blocks, user_weights, FBS_U)
    item_proj = project(y_vals, y_blocks, item_weights, FBS_I)

    def tile_step(item_total, triple):
        user_rows, rating_block, tile_row = triple
        rating_rows = rating_block.reshape(TILE, N_FEAT, N_ROWS, IS).transpose(0, 2, 1, 3).reshape(TILE, ITEMS)
        tile_mask = jnp.repeat(tile_row.astype(jnp.float32), TILE)
        predicted = jnp.dot(user_rows, item_proj.T, preferred_element_type=jnp.float32) * rank_scale
        residual = (tile_mask[None, :] * (predicted - rating_rows.astype(jnp.float32))).astype(jnp.bfloat16)
        user_grad_rows = (jnp.dot(residual, item_proj, preferred_element_type=jnp.float32) * grad_scale).astype(jnp.bfloat16)
        item_total = item_total + jnp.dot(residual.T, user_rows, preferred_element_type=jnp.float32)
        return (item_total, user_grad_rows)
    item_total = jnp.zeros((ITEMS, RANK), jnp.float32)
    item_total, user_grad_proj = lax.scan(tile_step, item_total, (user_proj.reshape(NUB, TILE, RANK), ratings.reshape(NUB, TILE, N_FEAT, N_ROWS * IS), observed))
    item_grad_proj = (item_total * grad_scale).astype(jnp.bfloat16)
    grad_user = block_grads(x_vals, x_blocks, user_grad_proj.reshape(-1, RANK), FBS_U)
    grad_item = block_grads(y_vals, y_blocks, item_grad_proj, FBS_I)
    return (grad_user, grad_item)
```

```python
import math

import jax
import jax.numpy as jnp
from jax import lax
from jax.experimental import pallas as pl
from jax.experimental.pallas import tpu as pltpu
from jax.sharding import PartitionSpec as P

TILE = 512
FBW = 128
RANK = 256
ROWS = 32
FEAT = 8
NX = 4
NZ = 4
K = 8
SH = TILE // FEAT
RP = RANK // ROWS
MESH = pl.DeviceIdType.MESH

IDX, A0, B0, C0, IZ, IX, IC, D0, DG0, EC, EX, EZ, FG, G0, NCH = (
    0, 1, 4, 7, 9, 10, 11, 12, 14, 16, 17, 18, 19, 20, 23)

NT = (((1,), (1,)), ((), ()))
NN = (((1,), (0,)), ((), ()))


def dot(a, b, dims):
    return lax.dot_general(a, b, dims, preferred_element_type=jnp.float32)


def kernel(idx_in, mask, wu_h, wi_h, x_h, y_h, rat_h, grecv, idx_all,
           wu, wi, wu3, wi3, xv, rat, idx_s, asend, arecv, wcat, part, rsr, share, upb,
           item_all, gacc, tacc, gpart, gpr, gshare, gfull, ebuf, ecr, es, exr,
           ez, ezr, gsend, upt, lsem, ssem, rsem):
    row = lax.axis_index("rows")
    feat = lax.axis_index("feat")
    mx = row // (2 * NZ)
    mz = lax.rem(row // 2, NZ)
    mc = lax.rem(row, 2)
    rank_scale = 1.0 / math.sqrt(RANK)
    grad_scale = 1.0 / (TILE * math.sqrt(RANK))

    def row_of(dx, dz, dc):
        return (lax.rem(mx + dx, NX) * (2 * NZ) + lax.rem(mz + dz, NZ) * 2
                + lax.rem(mc + dc, 2))

    def row_peer(j):
        return row_of(lax.rem(j // NZ, NX), lax.rem(j, NZ), j // (NX * NZ))

    def feat_peer(j):
        return lax.rem(feat + j, FEAT)

    def send(src, dst, ch, rows=None, f=None):
        pltpu.make_async_remote_copy(
            src_ref=src, dst_ref=dst, send_sem=ssem.at[ch], recv_sem=rsem.at[ch],
            device_id={"rows": row if rows is None else rows, "feat": feat if f is None else f},
            device_id_type=MESH).start()

    def bulk(ref, ch):
        return pltpu.make_async_remote_copy(
            src_ref=ref, dst_ref=ref, send_sem=ssem.at[ch], recv_sem=rsem.at[ch],
            device_id={"rows": row_of(0, 0, 1), "feat": feat}, device_id_type=MESH)

    loads = [
        pltpu.make_async_copy(wi_h, wi, lsem.at[0]),
        pltpu.make_async_copy(wu_h, wu, lsem.at[1]),
        pltpu.make_async_copy(y_h, xv.at[pl.ds(0, K)], lsem.at[2]),
        pltpu.make_async_copy(x_h, xv.at[pl.ds(K, 2 * K)], lsem.at[3]),
        pltpu.make_async_copy(rat_h, rat, lsem.at[4]),
    ]
    for c in loads:
        c.start()
    for c, table, blocks in ((loads[0], wi, wi3), (loads[1], wu, wu3)):
        c.wait()
        for i in range(blocks.shape[0]):
            blocks[i] = table[:, i * FBW:(i + 1) * FBW]

    barrier = pltpu.get_barrier_semaphore()

    @pl.loop(1, ROWS)
    def _(j):
        pl.semaphore_signal(barrier, inc=1, device_id={"rows": row_peer(j), "feat": feat},
                            device_id_type=MESH)

    @pl.loop(1, FEAT)
    def _(j):
        pl.semaphore_signal(barrier, inc=1, device_id={"rows": row, "feat": feat_peer(j)},
                            device_id_type=MESH)
    pl.semaphore_wait(barrier, ROWS - 1 + FEAT - 1)

    @pl.loop(1, ROWS)
    def _(j):
        send(idx_in.at[0], idx_all.at[row], IDX, rows=row_peer(ROWS - j))
    idx_all[row] = idx_in[0]
    bulk(idx_all.at[pl.ds(0, ROWS - 1)], IDX).wait_recv()
    to_smem = pltpu.make_async_copy(idx_all, idx_s, lsem.at[5])
    to_smem.start()
    to_smem.wait()

    def pick(table, dst, d, unit):
        for k in range(K):
            dst[k] = table[idx_s[d, 0, unit * K + k]]

    for unit in range(3):
        table = wi3 if unit == 0 else wu3

        @pl.loop(1, ROWS)
        def _(j):
            d = row_peer(ROWS - j)
            pick(table, asend.at[unit, d], d, unit)
            send(asend.at[unit, d], arecv.at[unit, row], A0 + unit, rows=d)
        pick(table, arecv.at[unit, row], row, unit)

    for c in loads[2:]:
        c.wait()

    def project(unit):
        bulk(arecv.at[unit, pl.ds(0, ROWS - 1)], A0 + unit).wait_recv()
        for k in range(K):
            w = arecv[unit, :, k].astype(jnp.float32).reshape(RANK, FBW)
            wcat[:, k * FBW:(k + 1) * FBW] = w.astype(jnp.bfloat16)
        half = FEAT // 2
        for h in range(2):
            xt = jnp.concatenate(
                [xv[unit * K + k, h * half * SH:(h + 1) * half * SH] for k in range(K)], axis=1)
            p = dot(xt, wcat[...], NT)
            part[unit, h * half:(h + 1) * half] = p.astype(jnp.bfloat16).reshape(half, SH, RANK)

    def scatter(src, dst, ch):
        @pl.loop(1, FEAT)
        def _(j):
            f = feat_peer(FEAT - j)
            send(src.at[f], dst.at[feat], ch, f=f)
        dst[feat] = src[feat]

    def summed(dst, ch):
        bulk(dst.at[pl.ds(0, FEAT - 1)], ch).wait_recv()
        total = dst[0].astype(jnp.float32)
        for f in range(1, FEAT):
            total = total + dst[f].astype(jnp.float32)
        return total.astype(jnp.bfloat16)

    def gather(src, dst, ch):
        @pl.loop(1, FEAT)
        def _(j):
            send(src, dst.at[feat], ch, f=feat_peer(FEAT - j))
        dst[feat] = src[...]

    def wait_gather(dst, ch):
        bulk(dst.at[pl.ds(0, FEAT - 1)], ch).wait_recv()

    def residual(b):
        up = upb[b].reshape(TILE, RANK)
        upt[...] = up.T
        gacc[...] = jnp.zeros_like(gacc)

        @pl.loop(0, 2 * NX)
        def _(q):
            x = q // 2
            z = lax.rem(q, 2) * 2
            it = jnp.concatenate(
                [item_all[c, x, z + dz] for dz in range(2) for c in range(2)], axis=0)
            cols = pl.ds(pl.multiple_of(q * RANK, RANK), RANK)
            pred = dot(upb[b].reshape(TILE, RANK), it, NT) * rank_scale
            r = mask[b:b + 1, cols] * (
                pred - rat[b * TILE:(b + 1) * TILE, cols].astype(jnp.float32))
            r = r.astype(jnp.bfloat16)
            gacc[...] += dot(r, it, NN)
            t = dot(upt[...], r, NN)
            if b == 0:
                tacc[:, cols] = t
            else:
                tacc[:, cols] += t
        gpart[b] = (gacc[...] * grad_scale).astype(jnp.bfloat16).reshape(FEAT, SH, RANK)

    def block_grads(unit):
        gt = gfull[unit].reshape(TILE, RANK).T
        for k in range(0, K, 2):
            two = jnp.concatenate([xv[unit * K + k], xv[unit * K + k + 1]], axis=1)
            o = dot(gt, two, NN)
            for i in range(2):
                s = o[:, i * FBW:(i + 1) * FBW].reshape(ROWS, RP, FBW)
                gsend[unit, :, k + i] = s.astype(jnp.bfloat16)

        @pl.loop(1, ROWS)
        def _(j):
            d = row_peer(ROWS - j)
            send(gsend.at[unit, d], grecv.at[unit, row], G0 + unit, rows=d)
        grecv[unit, row] = gsend[unit, row]

    project(0)
    scatter(part.at[0], rsr.at[0], B0)
    share[0] = summed(rsr.at[0], B0)
    item_all[mc, mx, mz] = share[0]
    for dz in (2, 1, 3):
        send(share.at[0], item_all.at[mc, mx, mz], IZ, rows=row_of(0, dz, 0))
    bulk(item_all.at[0, 0, pl.ds(0, NZ - 1)], IZ).wait_recv()
    for dx in (2, 1, 3):
        send(item_all.at[mc, mx], item_all.at[mc, mx], IX, rows=row_of(dx, 0, 0))
    bulk(item_all.at[0, pl.ds(0, NX - 1)], IX).wait_recv()
    send(item_all.at[mc], item_all.at[mc], IC, rows=row_of(0, 0, 1))

    project(1)
    scatter(part.at[1], rsr.at[1], B0 + 1)
    share[1] = summed(rsr.at[1], B0 + 1)
    gather(share.at[1], upb.at[0], C0)
    bulk(item_all.at[0], IC).wait_recv()
    wait_gather(upb.at[0], C0)
    residual(0)
    scatter(gpart.at[0], gpr.at[0], D0)

    project(2)
    scatter(part.at[2], rsr.at[2], B0 + 2)
    gshare[1] = summed(gpr.at[0], D0)
    gather(gshare.at[1], gfull.at[1], DG0)
    share[2] = summed(rsr.at[2], B0 + 2)
    gather(share.at[2], upb.at[1], C0 + 1)
    wait_gather(gfull.at[1], DG0)
    block_grads(1)
    wait_gather(upb.at[1], C0 + 1)
    residual(1)
    scatter(gpart.at[1], gpr.at[1], D0 + 1)

    @pl.loop(0, 2 * NX)
    def _(q):
        x = q // 2
        z = lax.rem(q, 2) * 2
        cols = pl.ds(pl.multiple_of(q * RANK, RANK), RANK)
        t = (tacc[:, cols] * grad_scale).T.astype(jnp.bfloat16)
        for dz in range(2):
            for c in range(2):
                i = dz * 2 + c
                ebuf[c, x, z + dz] = t[i * SH:(i + 1) * SH]
    send(ebuf.at[1 - mc], ecr, EC, rows=row_of(0, 0, 1))
    gshare[2] = summed(gpr.at[1], D0 + 1)
    gather(gshare.at[2], gfull.at[2], DG0 + 1)
    bulk(ecr, EC).wait_recv()

    @pl.loop(0, NX)
    def _(x):
        es[x] = (ebuf[mc, x].astype(jnp.float32)
                 + ecr[x].astype(jnp.float32)).astype(jnp.bfloat16)
    for dx in (2, 1, 3):
        x = lax.rem(mx + dx, NX)
        send(es.at[x], exr.at[mx], EX, rows=row_of(dx, 0, 0))
    exr[mx] = es[mx]
    wait_gather(gfull.at[2], DG0 + 1)
    block_grads(2)
    bulk(exr.at[pl.ds(0, NX - 1)], EX).wait_recv()
    for z in range(NZ):
        total = exr[0, z].astype(jnp.float32)
        for x in range(1, NX):
            total = total + exr[x, z].astype(jnp.float32)
        ez[z] = total.astype(jnp.bfloat16)
    for dz in (2, 1, 3):
        z = lax.rem(mz + dz, NZ)
        send(ez.at[z], ezr.at[mz], EZ, rows=row_of(0, dz, 0))
    ezr[mz] = ez[mz]
    bulk(ezr.at[pl.ds(0, NZ - 1)], EZ).wait_recv()
    total = ezr[0].astype(jnp.float32)
    for z in range(1, NZ):
        total = total + ezr[z].astype(jnp.float32)
    gshare[0] = total.astype(jnp.bfloat16)
    gather(gshare.at[0], gfull.at[0], FG)
    wait_gather(gfull.at[0], FG)
    block_grads(0)

    for u in (1, 2, 0):
        bulk(grecv.at[u, pl.ds(0, ROWS - 1)], G0 + u).wait_recv()

    bulk(idx_all.at[pl.ds(0, ROWS - 1)], IDX).wait_send()
    for u in range(3):
        bulk(asend.at[u, pl.ds(0, ROWS - 1)], A0 + u).wait_send()
        bulk(rsr.at[u, pl.ds(0, FEAT - 1)], B0 + u).wait_send()
        bulk(gsend.at[u, pl.ds(0, ROWS - 1)], G0 + u).wait_send()
    for b in range(2):
        bulk(upb.at[b, pl.ds(0, FEAT - 1)], C0 + b).wait_send()
        bulk(gpr.at[b, pl.ds(0, FEAT - 1)], D0 + b).wait_send()
        bulk(gfull.at[b, pl.ds(0, FEAT - 1)], DG0 + b).wait_send()
    bulk(item_all.at[0, 0, pl.ds(0, NZ - 1)], IZ).wait_send()
    bulk(item_all.at[0, pl.ds(0, NX - 1)], IX).wait_send()
    bulk(item_all.at[0], IC).wait_send()
    bulk(ecr, EC).wait_send()
    bulk(exr.at[pl.ds(0, NX - 1)], EX).wait_send()
    bulk(ezr.at[pl.ds(0, NZ - 1)], EZ).wait_send()
    bulk(gfull.at[0, pl.ds(0, FEAT - 1)], FG).wait_send()


def accumulate(returned, ids, blocks):
    onehot = (ids.reshape(-1)[:, None] == jnp.arange(blocks, dtype=jnp.int32)[None, :])
    totals = jnp.einsum("prc,pn->rnc", returned.reshape(-1, RP, FBW),
                        onehot.astype(jnp.bfloat16), preferred_element_type=jnp.float32)
    return totals.reshape(RP, blocks * FBW)


def on_device(x_vals, x_blocks, y_vals, y_blocks, user_weights, item_weights, observed, ratings):
    ids = jnp.concatenate([y_blocks.reshape(-1), x_blocks.reshape(-1)])
    ids = jnp.pad(ids, (0, FBW - 3 * K)).reshape(1, 1, FBW)
    mask = jnp.repeat(observed.astype(jnp.float32), SH, axis=1)
    bf, f32 = jnp.bfloat16, jnp.float32
    V = pltpu.VMEM
    grecv, idx_all = pl.pallas_call(
        kernel,
        out_shape=(jax.ShapeDtypeStruct((3, ROWS, K, RP, FBW), bf),
                   jax.ShapeDtypeStruct((ROWS, 1, FBW), jnp.int32)),
        in_specs=[pl.BlockSpec(memory_space=pltpu.VMEM)] * 2
        + [pl.BlockSpec(memory_space=pl.ANY)] * 5,
        out_specs=[pl.BlockSpec(memory_space=pltpu.VMEM)] * 2,
        scratch_shapes=[
            V(user_weights.shape, bf), V(item_weights.shape, bf),
            V((user_weights.shape[1] // FBW, RP, FBW), bf),
            V((item_weights.shape[1] // FBW, RP, FBW), bf), V((3 * K, TILE, FBW), bf),
            V((2 * TILE, ROWS * SH), bf), pltpu.SMEM((ROWS, 1, FBW), jnp.int32),
            V((3, ROWS, K, RP, FBW), bf), V((3, ROWS, K, RP, FBW), bf), V((RANK, K * FBW), bf),
            V((3, FEAT, SH, RANK), bf), V((3, FEAT, SH, RANK), bf), V((3, SH, RANK), bf),
            V((2, FEAT, SH, RANK), bf), V((2, NX, NZ, SH, RANK), bf), V((TILE, RANK), f32),
            V((RANK, ROWS * SH), f32), V((2, FEAT, SH, RANK), bf), V((2, FEAT, SH, RANK), bf),
            V((3, SH, RANK), bf), V((3, FEAT, SH, RANK), bf), V((2, NX, NZ, SH, RANK), bf),
            V((NX, NZ, SH, RANK), bf), V((NX, NZ, SH, RANK), bf), V((NX, NZ, SH, RANK), bf),
            V((NZ, SH, RANK), bf), V((NZ, SH, RANK), bf), V((3, ROWS, K, RP, FBW), bf),
            V((RANK, TILE), bf), pltpu.SemaphoreType.DMA((6,)),
            pltpu.SemaphoreType.DMA((NCH,)), pltpu.SemaphoreType.DMA((NCH,)),
        ],
        compiler_params=pltpu.CompilerParams(
            collective_id=0, has_side_effects=True),
        name="step",
    )(ids, mask, user_weights, item_weights, x_vals.reshape(2 * K, TILE, FBW),
      y_vals.reshape(K, TILE, FBW), ratings.reshape(2 * TILE, ROWS * SH))
    ids_all = idx_all[:, 0, :3 * K].reshape(ROWS, 3, K).swapaxes(0, 1)
    return (accumulate(grecv[1:], ids_all[1:], user_weights.shape[1] // FBW),
            accumulate(grecv[0], ids_all[0], item_weights.shape[1] // FBW))


def solution(mesh):
    return jax.shard_map(
        on_device,
        mesh=mesh,
        in_specs=(
            P("rows", "feat", None, None, None),
            P("rows", "feat", None),
            P("rows", "feat", None, None, None),
            P("rows", "feat", None),
            P("rows", "feat"),
            P("rows", "feat"),
            P("rows", None),
            P("rows", "feat", None),
        ),
        out_specs=(P("rows", "feat"), P("rows", "feat")),
        check_vma=False,
    )
```

```python
import math

import jax
import jax.numpy as jnp
from jax import lax
from jax.experimental import pallas as pl
from jax.experimental.pallas import tpu as pltpu
from jax.sharding import PartitionSpec as P

TILE = 512
FBW = 128
RANK = 256
ROWS = 32
FEAT = 8
NX = 4
NZ = 4
K = 8
SH = TILE // FEAT
NY = FEAT // 2
RP = RANK // ROWS
MESH = pl.DeviceIdType.MESH

IDX, A0, BY, BL, IZ, IX, IC, EC, EX, EZ, FL, FY, G0, UY, UL, UG, NCH = (
    0, 1, 4, 5, 6, 7, 8, 9, 10, 11, 12, 13, 14, 17, 21, 25, 29)

NT = (((1,), (1,)), ((), ()))
NN = (((1,), (0,)), ((), ()))


def dot(a, b, dims):
    return lax.dot_general(a, b, dims, preferred_element_type=jnp.float32)


def kernel(x_idx, y_idx, observed, wu_h, wi_h, x_h, y_h, rat_h, gru, gri, idx_all,
           wu, wi, wu3, wi3, xv, rat, mask, idx_loc, idx_s, asend, arecv, wcat, ipart,
           iyr, iys, ilr, ishare, apart, ayr, ays, alr, full, item_all, resid, tacc,
           ebuf, ecr, es, exr, ez, ezr, ifull, gsend, upt, lsem, ssem, rsem):
    row = lax.axis_index("rows")
    feat = lax.axis_index("feat")
    mx = row // (2 * NZ)
    mz = lax.rem(row // 2, NZ)
    mc = lax.rem(row, 2)
    my = feat // 2
    ml = lax.rem(feat, 2)
    bf, f32 = jnp.bfloat16, jnp.float32
    rank_scale = 1.0 / math.sqrt(RANK)
    grad_scale = 1.0 / (TILE * math.sqrt(RANK))

    def row_of(dx, dz, dc):
        return (lax.rem(mx + dx, NX) * (2 * NZ) + lax.rem(mz + dz, NZ) * 2
                + lax.rem(mc + dc, 2))

    def row_peer(j):
        return row_of(lax.rem(j // NZ, NX), lax.rem(j, NZ), j // (NX * NZ))

    def feat_of(dy, dl):
        return lax.rem(my + dy, NY) * 2 + lax.rem(ml + dl, 2)

    def copy(src, dst, ch, rows=None, f=None):
        return pltpu.make_async_remote_copy(
            src_ref=src, dst_ref=dst, send_sem=ssem.at[ch], recv_sem=rsem.at[ch],
            device_id={"rows": row if rows is None else rows, "feat": feat if f is None else f},
            device_id_type=MESH)

    unsent = []

    def send(src, dst, ch, rows=None, f=None):
        copy(src, dst, ch, rows, f).start()

    def arrived(ref, ch):
        c = copy(ref, ref, ch, rows=row_of(0, 0, 1))
        c.wait_recv()
        unsent.append(c)

    barrier = pltpu.get_barrier_semaphore()

    @pl.loop(1, ROWS)
    def _(j):
        pl.semaphore_signal(barrier, inc=1, device_id={"rows": row_peer(ROWS - j), "feat": feat},
                            device_id_type=MESH)
    feat_peers = [(0, 1)] + [(dy, 0) for dy in (2, 1, 3)]
    for dy, dl in feat_peers:
        pl.semaphore_signal(barrier, inc=1, device_id={"rows": row, "feat": feat_of(dy, dl)},
                            device_id_type=MESH)

    loads = [
        pltpu.make_async_copy(wi_h, wi, lsem.at[0]),
        pltpu.make_async_copy(wu_h, wu, lsem.at[1]),
        pltpu.make_async_copy(y_h, xv.at[pl.ds(0, K)], lsem.at[2]),
        pltpu.make_async_copy(x_h, xv.at[pl.ds(K, 2 * K)], lsem.at[3]),
        pltpu.make_async_copy(rat_h, rat, lsem.at[4]),
    ]
    for c in loads:
        c.start()
    idx_loc[...] = jnp.zeros_like(idx_loc)
    idx_loc[0:1, 0:K] = y_idx[...]
    idx_loc[1:3, 0:K] = x_idx[...]
    left = lax.broadcasted_iota(jnp.int32, (1, 2 * SH), 1) < SH
    for b in range(2):
        for p in range(ROWS // 2):
            pair = jnp.where(left, observed[b, 2 * p], observed[b, 2 * p + 1])
            mask[b:b + 1, p * 2 * SH:(p + 1) * 2 * SH] = pair.astype(f32)
    for c, table, blocks in ((loads[0], wi, wi3), (loads[1], wu, wu3)):
        c.wait()
        for i in range(blocks.shape[0]):
            blocks[i] = table[:, i * FBW:(i + 1) * FBW]
    pl.semaphore_wait(barrier, ROWS - 1 + len(feat_peers))

    @pl.loop(1, ROWS)
    def _(j):
        send(idx_loc, idx_all.at[row], IDX, rows=row_peer(ROWS - j))
    idx_all[row] = idx_loc[...]
    arrived(idx_all.at[pl.ds(0, ROWS - 1)], IDX)
    to_smem = pltpu.make_async_copy(idx_all, idx_s, lsem.at[5])
    to_smem.start()
    to_smem.wait()

    def pick(unit, dst, d):
        table = wi3 if unit == 0 else wu3
        for k in range(K):
            dst[k] = table[idx_s[d, unit, k]]

    def ask(unit, lo, hi, picks=True, sends=True):
        @pl.loop(lo, hi)
        def _(j):
            d = row_peer(ROWS - j)
            if picks:
                pick(unit, asend.at[unit, d], d)
            if sends:
                send(asend.at[unit, d], arecv.at[unit, row], A0 + unit, rows=d)

    def project(unit, dst):
        arrived(arecv.at[unit, pl.ds(0, ROWS - 1)], A0 + unit)
        for k in range(K):
            w = arecv[unit, :, k].astype(f32).reshape(RANK, FBW)
            wcat[:, k * FBW:(k + 1) * FBW] = w.astype(bf)
        half = TILE // 2
        for h in range(2):
            xt = jnp.concatenate(
                [xv[unit * K + k, h * half:(h + 1) * half] for k in range(K)], axis=1)
            p = dot(xt, wcat[...], NT)
            dst[h * 2:(h + 1) * 2] = p.astype(bf).reshape(2, 2, SH, RANK)

    def y_scatter(src, dst, ch):
        for dy in (2, 1, 3):
            y = lax.rem(my + dy, NY)
            send(src.at[y], dst.at[my], ch, f=feat_of(dy, 0))
        dst[my] = src[my]

    def y_sum(dst, out, ch):
        arrived(dst.at[pl.ds(0, NY - 1)], ch)
        for l in range(2):
            total = dst[0, l].astype(f32)
            for y in range(1, NY):
                total = total + dst[y, l].astype(f32)
            out[l] = total.astype(bf)

    def y_gather(dst, ch):
        for dy in (2, 1, 3):
            send(dst.at[my], dst.at[my], ch, f=feat_of(dy, 0))

    def y_full(dst, ch):
        arrived(dst.at[pl.ds(0, NY - 1)], ch)

    def s_send(i):
        y_scatter(apart.at[i], ayr.at[i], UY + i)

    def s_mid(i):
        y_sum(ayr.at[i], ays.at[i], UY + i)
        send(ays.at[i], alr.at[i], UL + i, f=feat_of(0, 1))

    def s_out(i):
        arrived(alr.at[i], UL + i)
        full[i, my] = (ays[i].astype(f32) + alr[i].astype(f32)).astype(bf)
        y_gather(full.at[i], UG + i)

    def s_wait(i):
        y_full(full.at[i], UG + i)

    def residual(b):
        upt[...] = full[b].reshape(TILE, RANK).T

        @pl.loop(0, NX)
        def _(x):
            it = item_all[x].reshape(2 * TILE // 2, RANK)
            cols = pl.ds(pl.multiple_of(x * TILE, TILE), TILE)
            pred = dot(full[b].reshape(TILE, RANK), it, NT) * rank_scale
            r = mask[b:b + 1, cols] * (pred - rat[b * TILE:(b + 1) * TILE, cols].astype(f32))
            r = r.astype(bf)
            resid[:, cols] = r
            t = dot(upt[...], r, NN)
            if b == 0:
                tacc[:, cols] = t
            else:
                tacc[:, cols] += t
        for h in range(2):
            g = dot(resid[h * RANK:(h + 1) * RANK, :], item_all[...].reshape(ROWS * SH, RANK), NN)
            apart[2 + b, h * 2:(h + 1) * 2] = (g * grad_scale).astype(bf).reshape(2, 2, SH, RANK)

    def block_grads(unit, src, out):
        gt = src[...].reshape(TILE, RANK).T
        for k in range(0, K, 2):
            two = jnp.concatenate([xv[unit * K + k], xv[unit * K + k + 1]], axis=1)
            o = dot(gt, two, NN)
            for i in range(2):
                s = o[:, i * FBW:(i + 1) * FBW].reshape(ROWS, RP, FBW)
                gsend[unit, :, k + i] = s.astype(bf)
        out[row] = gsend[unit, row]

    def give(unit, out, lo, hi):
        @pl.loop(lo, hi)
        def _(j):
            d = row_peer(ROWS - j)
            send(gsend.at[unit, d], out.at[row], G0 + unit, rows=d)

    ask(0, 1, ROWS)
    ask(1, 1, ROWS)
    for unit in range(3):
        pick(unit, arecv.at[unit, row], row)
    for c in loads[2:]:
        c.wait()
    project(0, ipart)
    y_scatter(ipart, iyr, BY)
    ask(2, 1, ROWS, sends=False)
    y_sum(iyr, iys, BY)
    send(iys.at[1 - ml], ilr, BL, f=feat_of(0, 1))
    ask(2, 1, HALF, picks=False)
    project(1, apart.at[0])
    s_send(0)
    arrived(ilr, BL)
    ishare[...] = (iys[ml].astype(f32) + ilr[...].astype(f32)).astype(bf)
    item_all[mx, mz, mc] = ishare[...]
    for dz in (2, 1, 3):
        send(ishare, item_all.at[mx, mz, mc], IZ, rows=row_of(0, dz, 0))
    ask(2, HALF, ROWS, picks=False)
    s_mid(0)
    arrived(item_all.at[0, pl.ds(0, NZ - 1), 0], IZ)
    for dx in (2, 1, 3):
        send(item_all.at[mx, :, mc], item_all.at[mx, :, mc], IX, rows=row_of(dx, 0, 0))
    s_out(0)
    arrived(item_all.at[pl.ds(0, NX - 1), :, 0], IX)
    send(item_all.at[:, :, mc], item_all.at[:, :, mc], IC, rows=row_of(0, 0, 1))
    project(2, apart.at[1])
    s_send(1)
    arrived(item_all.at[:, :, 0], IC)
    s_wait(0)
    residual(0)
    s_send(2)
    s_mid(1)
    s_out(1)
    s_mid(2)
    s_out(2)
    s_wait(1)
    residual(1)
    s_send(3)
    s_wait(2)
    block_grads(1, full.at[2], gru.at[0])
    give(1, gru.at[0], 1, HALF)

    for q in range(2 * NX):
        t = (tacc[:, q * RANK:(q + 1) * RANK] * grad_scale).T.astype(bf)
        for i in range(4):
            g = q * 4 + i
            ebuf[g // (2 * NZ), (g // 2) % NZ, g % 2] = t[i * SH:(i + 1) * SH]
    send(ebuf.at[:, :, 1 - mc], ecr, EC, rows=row_of(0, 0, 1))
    s_mid(3)
    give(1, gru.at[0], HALF, ROWS)
    arrived(ecr, EC)

    @pl.loop(0, NX)
    def _(x):
        es[x] = (ebuf[x, :, mc].astype(f32) + ecr[x].astype(f32)).astype(bf)
    for dx in (2, 1, 3):
        send(es.at[lax.rem(mx + dx, NX)], exr.at[mx], EX, rows=row_of(dx, 0, 0))
    exr[mx] = es[mx]
    s_out(3)
    arrived(exr.at[pl.ds(0, NX - 1)], EX)
    for z in range(NZ):
        total = exr[0, z].astype(f32)
        for x in range(1, NX):
            total = total + exr[x, z].astype(f32)
        ez[z] = total.astype(bf)
    for dz in (2, 1, 3):
        send(ez.at[lax.rem(mz + dz, NZ)], ezr.at[mz], EZ, rows=row_of(0, dz, 0))
    ezr[mz] = ez[mz]
    s_wait(3)
    block_grads(2, full.at[3], gru.at[1])
    give(2, gru.at[1], 1, HALF)
    arrived(ezr.at[pl.ds(0, NZ - 1)], EZ)
    total = ezr[0].astype(f32)
    for z in range(1, NZ):
        total = total + ezr[z].astype(f32)
    ishare2 = total.astype(bf)
    ifull[my, ml] = ishare2
    send(ifull.at[my, ml], ifull.at[my, ml], FL, f=feat_of(0, 1))
    give(2, gru.at[1], HALF, ROWS)
    arrived(ifull.at[0, 0], FL)
    y_gather(ifull, FY)
    y_full(ifull, FY)
    block_grads(0, ifull, gri)
    give(0, gri, 1, ROWS)

    arrived(gru.at[0, pl.ds(0, ROWS - 1)], G0 + 1)
    arrived(gru.at[1, pl.ds(0, ROWS - 1)], G0 + 2)
    arrived(gri.at[pl.ds(0, ROWS - 1)], G0)
    for c in unsent:
        c.wait_send()


HALF = ROWS // 2


def accumulate(returned, ids, blocks):
    onehot = (ids.reshape(-1)[:, None] == jnp.arange(blocks, dtype=jnp.int32)[None, :])
    totals = jnp.einsum("prc,pn->rnc", returned.reshape(-1, RP, FBW),
                        onehot.astype(jnp.bfloat16), preferred_element_type=jnp.float32)
    return totals.reshape(RP, blocks * FBW)


def on_device(x_vals, x_blocks, y_vals, y_blocks, user_weights, item_weights, observed, ratings):
    bf, f32 = jnp.bfloat16, jnp.float32
    V = pltpu.VMEM
    n_u, n_i = user_weights.shape[1] // FBW, item_weights.shape[1] // FBW
    slab = (SH, RANK)
    items = (NX, NZ, 2, SH, RANK)
    gru, gri, idx_all = pl.pallas_call(
        kernel,
        out_shape=(jax.ShapeDtypeStruct((2, ROWS, K, RP, FBW), bf),
                   jax.ShapeDtypeStruct((ROWS, K, RP, FBW), bf),
                   jax.ShapeDtypeStruct((ROWS, 4, FBW), jnp.int32)),
        in_specs=[pl.BlockSpec(memory_space=pltpu.VMEM)] * 2
        + [pl.BlockSpec(memory_space=pltpu.SMEM)]
        + [pl.BlockSpec(memory_space=pl.ANY)] * 5,
        out_specs=[pl.BlockSpec(memory_space=pltpu.VMEM)] * 3,
        scratch_shapes=[
            V(user_weights.shape, bf), V(item_weights.shape, bf),
            V((n_u, RP, FBW), bf), V((n_i, RP, FBW), bf),
            V((3 * K, TILE, FBW), bf), V((2 * TILE, ROWS * SH), bf), V((2, ROWS * SH), f32),
            V((4, FBW), jnp.int32), pltpu.SMEM((ROWS, 4, FBW), jnp.int32),
            V((3, ROWS, K, RP, FBW), bf), V((3, ROWS, K, RP, FBW), bf), V((RANK, K * FBW), bf),
            V((NY, 2, *slab), bf), V((NY, 2, *slab), bf), V((2, *slab), bf), V(slab, bf), V(slab, bf),
            V((4, NY, 2, *slab), bf), V((4, NY, 2, *slab), bf), V((4, 2, *slab), bf),
            V((4, 2, *slab), bf), V((4, NY, 2, *slab), bf),
            V(items, bf), V((TILE, ROWS * SH), bf), V((RANK, ROWS * SH), f32),
            V(items, bf), V((NX, NZ, *slab), bf), V((NX, NZ, *slab), bf), V((NX, NZ, *slab), bf),
            V((NZ, *slab), bf), V((NZ, *slab), bf), V((NY, 2, *slab), bf),
            V((3, ROWS, K, RP, FBW), bf), V((RANK, TILE), bf), pltpu.SemaphoreType.DMA((6,)),
            pltpu.SemaphoreType.DMA((NCH,)), pltpu.SemaphoreType.DMA((NCH,)),
        ],
        compiler_params=pltpu.CompilerParams(collective_id=0, has_side_effects=True),
        name="step",
    )(x_blocks.reshape(2, K), y_blocks.reshape(1, K), observed, user_weights, item_weights,
      x_vals.reshape(2 * K, TILE, FBW), y_vals.reshape(K, TILE, FBW),
      ratings.reshape(2 * TILE, ROWS * SH))
    return (accumulate(gru, idx_all[:, 1:3, :K].swapaxes(0, 1), n_u),
            accumulate(gri, idx_all[:, 0, :K], n_i))


def solution(mesh):
    return jax.shard_map(
        on_device,
        mesh=mesh,
        in_specs=(
            P("rows", "feat", None, None, None),
            P("rows", "feat", None),
            P("rows", "feat", None, None, None),
            P("rows", "feat", None),
            P("rows", "feat"),
            P("rows", "feat"),
            P("rows", None),
            P("rows", "feat", None),
        ),
        out_specs=(P("rows", "feat"), P("rows", "feat")),
        check_vma=False,
    )
```

```python
import math

import jax
import jax.numpy as jnp
from jax import lax
from jax.experimental import pallas as pl
from jax.experimental.pallas import tpu as pltpu
from jax.sharding import PartitionSpec as P

TILE = 512
FBW = 128
RANK = 256
ROWS = 32
FEAT = 8
NX = 4
NZ = 4
K = 8
SH = TILE // FEAT
NY = FEAT // 2
RP = RANK // ROWS
MESH = pl.DeviceIdType.MESH

IDX, A0, BY, BL, IZ, IX, IC, EC, EX, EZ, FL, FY, G0, UY, UL, UG, NCH = (
    0, 1, 4, 5, 6, 7, 8, 9, 10, 11, 12, 13, 14, 17, 21, 25, 29)

NT = (((1,), (1,)), ((), ()))
NN = (((1,), (0,)), ((), ()))


def dot(a, b, dims):
    return lax.dot_general(a, b, dims, preferred_element_type=jnp.float32)


def kernel(x_idx, y_idx, observed, wu_h, wi_h, x_h, y_h, rat_h, out_u, out_i,
           gru, gri, idx_all, ohu, ohi, acc, wu, wi, wu3, wi3, xv, rat, mask, idx_loc, idx_s, asend, arecv, wcat, ipart,
           iyr, iys, ilr, ishare, apart, ayr, ays, alr, full, item_all, resid, tacc,
           ebuf, ecr, es, exr, ez, ezr, ifull, gsend, upt, lsem, ssem, rsem):
    row = lax.axis_index("rows")
    feat = lax.axis_index("feat")
    mx = row // (2 * NZ)
    mz = lax.rem(row // 2, NZ)
    mc = lax.rem(row, 2)
    my = feat // 2
    ml = lax.rem(feat, 2)
    bf, f32 = jnp.bfloat16, jnp.float32
    rank_scale = 1.0 / math.sqrt(RANK)
    grad_scale = 1.0 / (TILE * math.sqrt(RANK))

    def row_of(dx, dz, dc):
        return (lax.rem(mx + dx, NX) * (2 * NZ) + lax.rem(mz + dz, NZ) * 2
                + lax.rem(mc + dc, 2))

    def row_peer(j):
        return row_of(lax.rem(j // NZ, NX), lax.rem(j, NZ), j // (NX * NZ))

    def feat_of(dy, dl):
        return lax.rem(my + dy, NY) * 2 + lax.rem(ml + dl, 2)

    def copy(src, dst, ch, rows=None, f=None):
        return pltpu.make_async_remote_copy(
            src_ref=src, dst_ref=dst, send_sem=ssem.at[ch], recv_sem=rsem.at[ch],
            device_id={"rows": row if rows is None else rows, "feat": feat if f is None else f},
            device_id_type=MESH)

    unsent = []

    def send(src, dst, ch, rows=None, f=None):
        copy(src, dst, ch, rows, f).start()

    def arrived(ref, ch):
        c = copy(ref, ref, ch, rows=row_of(0, 0, 1))
        c.wait_recv()
        unsent.append(c)

    barrier = pltpu.get_barrier_semaphore()

    @pl.loop(1, ROWS)
    def _(j):
        pl.semaphore_signal(barrier, inc=1, device_id={"rows": row_peer(ROWS - j), "feat": feat},
                            device_id_type=MESH)
    feat_peers = [(0, 1)] + [(dy, 0) for dy in (2, 1, 3)]
    for dy, dl in feat_peers:
        pl.semaphore_signal(barrier, inc=1, device_id={"rows": row, "feat": feat_of(dy, dl)},
                            device_id_type=MESH)

    loads = [
        pltpu.make_async_copy(wi_h, wi, lsem.at[0]),
        pltpu.make_async_copy(wu_h, wu, lsem.at[1]),
        pltpu.make_async_copy(y_h, xv.at[pl.ds(0, K)], lsem.at[2]),
        pltpu.make_async_copy(x_h, xv.at[pl.ds(K, 2 * K)], lsem.at[3]),
        pltpu.make_async_copy(rat_h, rat, lsem.at[4]),
    ]
    for c in loads:
        c.start()
    idx_loc[...] = jnp.zeros_like(idx_loc)
    idx_loc[0:1, 0:K] = y_idx[...]
    idx_loc[1:3, 0:K] = x_idx[...]
    left = lax.broadcasted_iota(jnp.int32, (1, 2 * SH), 1) < SH
    for b in range(2):
        for p in range(ROWS // 2):
            pair = jnp.where(left, observed[b, 2 * p], observed[b, 2 * p + 1])
            mask[b:b + 1, p * 2 * SH:(p + 1) * 2 * SH] = pair.astype(f32)
    for c, table, blocks in ((loads[0], wi, wi3), (loads[1], wu, wu3)):
        c.wait()
        for i in range(blocks.shape[0]):
            blocks[i] = table[:, i * FBW:(i + 1) * FBW]
    pl.semaphore_wait(barrier, ROWS - 1 + len(feat_peers))

    @pl.loop(1, ROWS)
    def _(j):
        send(idx_loc, idx_all.at[row], IDX, rows=row_peer(ROWS - j))
    idx_all[row] = idx_loc[...]
    arrived(idx_all.at[pl.ds(0, ROWS - 1)], IDX)
    to_smem = pltpu.make_async_copy(idx_all, idx_s, lsem.at[5])
    to_smem.start()
    to_smem.wait()

    def pick(unit, dst, d):
        table = wi3 if unit == 0 else wu3
        for k in range(K):
            dst[k] = table[idx_s[d, unit, k]]

    def ask(unit, lo, hi, picks=True, sends=True):
        @pl.loop(lo, hi)
        def _(j):
            d = row_peer(ROWS - j)
            if picks:
                pick(unit, asend.at[unit, d], d)
            if sends:
                send(asend.at[unit, d], arecv.at[unit, row], A0 + unit, rows=d)

    def project(unit, dst):
        arrived(arecv.at[unit, pl.ds(0, ROWS - 1)], A0 + unit)
        for k in range(K):
            w = arecv[unit, :, k].astype(f32).reshape(RANK, FBW)
            wcat[:, k * FBW:(k + 1) * FBW] = w.astype(bf)
        half = TILE // 2
        for h in range(2):
            xt = jnp.concatenate(
                [xv[unit * K + k, h * half:(h + 1) * half] for k in range(K)], axis=1)
            p = dot(xt, wcat[...], NT)
            dst[h * 2:(h + 1) * 2] = p.astype(bf).reshape(2, 2, SH, RANK)

    def y_scatter(src, dst, ch):
        for dy in (2, 1, 3):
            y = lax.rem(my + dy, NY)
            send(src.at[y], dst.at[my], ch, f=feat_of(dy, 0))
        dst[my] = src[my]

    def y_sum(dst, out, ch):
        arrived(dst.at[pl.ds(0, NY - 1)], ch)
        for l in range(2):
            total = dst[0, l].astype(f32)
            for y in range(1, NY):
                total = total + dst[y, l].astype(f32)
            out[l] = total.astype(bf)

    def y_gather(dst, ch):
        for dy in (2, 1, 3):
            send(dst.at[my], dst.at[my], ch, f=feat_of(dy, 0))

    def y_full(dst, ch):
        arrived(dst.at[pl.ds(0, NY - 1)], ch)

    def s_send(i):
        y_scatter(apart.at[i], ayr.at[i], UY + i)

    def s_mid(i):
        y_sum(ayr.at[i], ays.at[i], UY + i)
        send(ays.at[i], alr.at[i], UL + i, f=feat_of(0, 1))

    def s_out(i):
        arrived(alr.at[i], UL + i)
        full[i, my] = (ays[i].astype(f32) + alr[i].astype(f32)).astype(bf)
        y_gather(full.at[i], UG + i)

    def s_wait(i):
        y_full(full.at[i], UG + i)

    def residual(b):
        upt[...] = full[b].reshape(TILE, RANK).T

        @pl.loop(0, NX)
        def _(x):
            it = item_all[x].reshape(2 * TILE // 2, RANK)
            cols = pl.ds(pl.multiple_of(x * TILE, TILE), TILE)
            pred = dot(full[b].reshape(TILE, RANK), it, NT) * rank_scale
            r = mask[b:b + 1, cols] * (pred - rat[b * TILE:(b + 1) * TILE, cols].astype(f32))
            r = r.astype(bf)
            resid[:, cols] = r
            t = dot(upt[...], r, NN)
            if b == 0:
                tacc[:, cols] = t
            else:
                tacc[:, cols] += t
        for h in range(2):
            g = dot(resid[h * RANK:(h + 1) * RANK, :], item_all[...].reshape(ROWS * SH, RANK), NN)
            apart[2 + b, h * 2:(h + 1) * 2] = (g * grad_scale).astype(bf).reshape(2, 2, SH, RANK)

    def block_grads(unit, src, out):
        gt = src[...].reshape(TILE, RANK).T
        for k in range(0, K, 2):
            two = jnp.concatenate([xv[unit * K + k], xv[unit * K + k + 1]], axis=1)
            o = dot(gt, two, NN)
            for i in range(2):
                s = o[:, i * FBW:(i + 1) * FBW].reshape(ROWS, RP, FBW)
                gsend[unit, :, k + i] = s.astype(bf)
        out[row] = gsend[unit, row]

    def give(unit, out, lo, hi):
        @pl.loop(lo, hi)
        def _(j):
            d = row_peer(ROWS - j)
            send(gsend.at[unit, d], out.at[row], G0 + unit, rows=d)

    def onehots():
        for unit in range(3):
            ids = idx_all[:, unit]
            blocks = ohi.shape[0] if unit == 0 else ohu.shape[1]
            lanes = lax.broadcasted_iota(jnp.int32, (ROWS, blocks), 1)
            rows = [jnp.where(ids[:, k:k + 1] == lanes, 1.0, 0.0) for k in range(K)]
            hot = jnp.concatenate(rows, axis=0).T.astype(bf)
            if unit == 0:
                ohi[...] = hot
            else:
                ohu[unit - 1] = hot

    def accumulate(returned, hot, out, first):
        for k in range(K):
            acc[k * RANK:(k + 1) * RANK] = returned[:, k].astype(f32).reshape(RANK, FBW)
        blocks = out.shape[0] // RP
        for r in range(0, RP, 2):
            two = jnp.concatenate(
                [acc[pl.ds(r + i, ROWS * K, stride=RP)].astype(bf) for i in range(2)], axis=1)
            o = dot(hot[...], two, NN)
            for i in range(2):
                v = o[:blocks, i * FBW:(i + 1) * FBW]
                at = pl.ds(r + i, blocks, stride=RP)
                if first:
                    out[at] = v
                else:
                    out[at] += v

    ask(0, 1, ROWS)
    ask(1, 1, ROWS)
    for unit in range(3):
        pick(unit, arecv.at[unit, row], row)
    for c in loads[2:]:
        c.wait()
    project(0, ipart)
    y_scatter(ipart, iyr, BY)
    ask(2, 1, ROWS, sends=False)
    y_sum(iyr, iys, BY)
    send(iys.at[1 - ml], ilr, BL, f=feat_of(0, 1))
    ask(2, 1, 16, picks=False)
    onehots()
    project(1, apart.at[0])
    s_send(0)
    arrived(ilr, BL)
    ishare[...] = (iys[ml].astype(f32) + ilr[...].astype(f32)).astype(bf)
    item_all[mx, mz, mc] = ishare[...]
    for dz in (2, 1, 3):
        send(ishare, item_all.at[mx, mz, mc], IZ, rows=row_of(0, dz, 0))
    ask(2, 16, ROWS, picks=False)
    s_mid(0)
    arrived(item_all.at[0, pl.ds(0, NZ - 1), 0], IZ)
    for dx in (2, 1, 3):
        send(item_all.at[mx, :, mc], item_all.at[mx, :, mc], IX, rows=row_of(dx, 0, 0))
    s_out(0)
    arrived(item_all.at[pl.ds(0, NX - 1), :, 0], IX)
    send(item_all.at[:, :, mc], item_all.at[:, :, mc], IC, rows=row_of(0, 0, 1))
    project(2, apart.at[1])
    s_send(1)
    arrived(item_all.at[:, :, 0], IC)
    s_wait(0)
    residual(0)
    s_send(2)
    s_mid(1)
    s_out(1)
    s_mid(2)
    s_out(2)
    s_wait(1)
    residual(1)
    s_send(3)
    s_wait(2)
    block_grads(1, full.at[2], gru.at[0])
    give(1, gru.at[0], 1, 16)

    for q in range(2 * NX):
        t = (tacc[:, q * RANK:(q + 1) * RANK] * grad_scale).T.astype(bf)
        for i in range(4):
            g = q * 4 + i
            ebuf[g // (2 * NZ), (g // 2) % NZ, g % 2] = t[i * SH:(i + 1) * SH]
    send(ebuf.at[:, :, 1 - mc], ecr, EC, rows=row_of(0, 0, 1))
    s_mid(3)
    give(1, gru.at[0], 16, ROWS)
    arrived(ecr, EC)

    @pl.loop(0, NX)
    def _(x):
        es[x] = (ebuf[x, :, mc].astype(f32) + ecr[x].astype(f32)).astype(bf)
    for dx in (2, 1, 3):
        send(es.at[lax.rem(mx + dx, NX)], exr.at[mx], EX, rows=row_of(dx, 0, 0))
    exr[mx] = es[mx]
    s_out(3)
    arrived(exr.at[pl.ds(0, NX - 1)], EX)
    for z in range(NZ):
        total = exr[0, z].astype(f32)
        for x in range(1, NX):
            total = total + exr[x, z].astype(f32)
        ez[z] = total.astype(bf)
    for dz in (2, 1, 3):
        send(ez.at[lax.rem(mz + dz, NZ)], ezr.at[mz], EZ, rows=row_of(0, dz, 0))
    ezr[mz] = ez[mz]
    s_wait(3)
    block_grads(2, full.at[3], gru.at[1])
    give(2, gru.at[1], 1, 12)
    arrived(ezr.at[pl.ds(0, NZ - 1)], EZ)
    total = ezr[0].astype(f32)
    for z in range(1, NZ):
        total = total + ezr[z].astype(f32)
    ifull[my, ml] = total.astype(bf)
    send(ifull.at[my, ml], ifull.at[my, ml], FL, f=feat_of(0, 1))
    give(2, gru.at[1], 12, ROWS)
    arrived(ifull.at[0, 0], FL)
    y_gather(ifull, FY)
    y_full(ifull, FY)
    block_grads(0, ifull, gri)
    give(0, gri, 1, ROWS)

    arrived(gru.at[0, pl.ds(0, ROWS - 1)], G0 + 1)
    accumulate(gru.at[0], ohu.at[0], out_u, True)
    arrived(gru.at[1, pl.ds(0, ROWS - 1)], G0 + 2)
    accumulate(gru.at[1], ohu.at[1], out_u, False)
    arrived(gri.at[pl.ds(0, ROWS - 1)], G0)
    accumulate(gri, ohi, out_i, True)
    for c in unsent:
        c.wait_send()


def on_device(x_vals, x_blocks, y_vals, y_blocks, user_weights, item_weights, observed, ratings):
    bf, f32 = jnp.bfloat16, jnp.float32
    V = pltpu.VMEM
    n_u, n_i = user_weights.shape[1] // FBW, item_weights.shape[1] // FBW
    pad_u, pad_i = -(-n_u // FBW) * FBW, -(-n_i // FBW) * FBW
    slab = (SH, RANK)
    items = (NX, NZ, 2, SH, RANK)
    out_u, out_i = pl.pallas_call(
        kernel,
        out_shape=(jax.ShapeDtypeStruct((n_u * RP, FBW), f32),
                   jax.ShapeDtypeStruct((n_i * RP, FBW), f32)),
        in_specs=[pl.BlockSpec(memory_space=pltpu.VMEM)] * 2
        + [pl.BlockSpec(memory_space=pltpu.SMEM)]
        + [pl.BlockSpec(memory_space=pl.ANY)] * 5,
        out_specs=[pl.BlockSpec(memory_space=pltpu.VMEM)] * 2,
        scratch_shapes=[
            V((2, ROWS, K, RP, FBW), bf), V((ROWS, K, RP, FBW), bf), V((ROWS, 4, FBW), jnp.int32),
            V((2, pad_u, ROWS * K), bf), V((pad_i, ROWS * K), bf), V((K * RANK, FBW), f32),
            V(user_weights.shape, bf), V(item_weights.shape, bf),
            V((n_u, RP, FBW), bf), V((n_i, RP, FBW), bf),
            V((3 * K, TILE, FBW), bf), V((2 * TILE, ROWS * SH), bf), V((2, ROWS * SH), f32),
            V((4, FBW), jnp.int32), pltpu.SMEM((ROWS, 4, FBW), jnp.int32),
            V((3, ROWS, K, RP, FBW), bf), V((3, ROWS, K, RP, FBW), bf), V((RANK, K * FBW), bf),
            V((NY, 2, *slab), bf), V((NY, 2, *slab), bf), V((2, *slab), bf), V(slab, bf), V(slab, bf),
            V((4, NY, 2, *slab), bf), V((4, NY, 2, *slab), bf), V((4, 2, *slab), bf),
            V((4, 2, *slab), bf), V((4, NY, 2, *slab), bf),
            V(items, bf), V((TILE, ROWS * SH), bf), V((RANK, ROWS * SH), f32),
            V(items, bf), V((NX, NZ, *slab), bf), V((NX, NZ, *slab), bf), V((NX, NZ, *slab), bf),
            V((NZ, *slab), bf), V((NZ, *slab), bf), V((NY, 2, *slab), bf),
            V((3, ROWS, K, RP, FBW), bf), V((RANK, TILE), bf), pltpu.SemaphoreType.DMA((6,)),
            pltpu.SemaphoreType.DMA((NCH,)), pltpu.SemaphoreType.DMA((NCH,)),
        ],
        compiler_params=pltpu.CompilerParams(collective_id=0, has_side_effects=True),
        name="step",
    )(x_blocks.reshape(2, K), y_blocks.reshape(1, K), observed, user_weights, item_weights,
      x_vals.reshape(2 * K, TILE, FBW), y_vals.reshape(K, TILE, FBW),
      ratings.reshape(2 * TILE, ROWS * SH))
    return (out_u.reshape(n_u, RP, FBW).swapaxes(0, 1).reshape(user_weights.shape),
            out_i.reshape(n_i, RP, FBW).swapaxes(0, 1).reshape(item_weights.shape))


def solution(mesh):
    return jax.shard_map(
        on_device,
        mesh=mesh,
        in_specs=(
            P("rows", "feat", None, None, None),
            P("rows", "feat", None),
            P("rows", "feat", None, None, None),
            P("rows", "feat", None),
            P("rows", "feat"),
            P("rows", "feat"),
            P("rows", None),
            P("rows", "feat", None),
        ),
        out_specs=(P("rows", "feat"), P("rows", "feat")),
        check_vma=False,
    )
```

```python
import math

import jax
import jax.numpy as jnp
from jax import lax
from jax.experimental import pallas as pl
from jax.experimental.pallas import tpu as pltpu
from jax.sharding import PartitionSpec as P

TILE = 512
FBW = 128
RANK = 256
ROWS = 32
FEAT = 8
NX = 4
NZ = 4
K = 8
SH = TILE // FEAT
NY = FEAT // 2
RP = RANK // ROWS
MESH = pl.DeviceIdType.MESH
DIRECT = (1, 2)

IDX, A0, BY, BL, IZ, IX, IC, EC, EX, EZ, FL, FY, G0, UY, UL, UG, NCH = (
    0, 1, 4, 5, 6, 7, 8, 9, 10, 11, 12, 13, 14, 17, 21, 25, 29)

NT = (((1,), (1,)), ((), ()))
NN = (((1,), (0,)), ((), ()))


def dot(a, b, dims):
    return lax.dot_general(a, b, dims, preferred_element_type=jnp.float32)


def kernel(x_idx, y_idx, observed, wu_h, wi_h, x_h, y_h, rat_h, out_u, out_i,
           gru, gri, idx_all, ohu, ohi, acc, wu, wi, wu3, wi3, xv, rat, mask, idx_loc, idx_s, asend, arecv, wcat, ipart,
           iyr, iys, ilr, ishare, apart, ayr, ays, alr, full, item_all, resid, tacc,
           ebuf, ecr, es, exr, ez, ezr, ifull, gsend, upt, lsem, ssem, rsem):
    row = lax.axis_index("rows")
    feat = lax.axis_index("feat")
    mx = row // (2 * NZ)
    mz = lax.rem(row // 2, NZ)
    mc = lax.rem(row, 2)
    my = feat // 2
    ml = lax.rem(feat, 2)
    bf, f32 = jnp.bfloat16, jnp.float32
    rank_scale = 1.0 / math.sqrt(RANK)
    grad_scale = 1.0 / (TILE * math.sqrt(RANK))

    def row_of(dx, dz, dc):
        return (lax.rem(mx + dx, NX) * (2 * NZ) + lax.rem(mz + dz, NZ) * 2
                + lax.rem(mc + dc, 2))

    def row_peer(j):
        return row_of(lax.rem(j // NZ, NX), lax.rem(j, NZ), j // (NX * NZ))

    def feat_of(dy, dl):
        return lax.rem(my + dy, NY) * 2 + lax.rem(ml + dl, 2)

    def copy(src, dst, ch, rows=None, f=None):
        return pltpu.make_async_remote_copy(
            src_ref=src, dst_ref=dst, send_sem=ssem.at[ch], recv_sem=rsem.at[ch],
            device_id={"rows": row if rows is None else rows, "feat": feat if f is None else f},
            device_id_type=MESH)

    unsent = []

    def send(src, dst, ch, rows=None, f=None):
        copy(src, dst, ch, rows, f).start()

    def arrived(ref, ch):
        c = copy(ref, ref, ch, rows=row_of(0, 0, 1))
        c.wait_recv()
        unsent.append(c)

    barrier = pltpu.get_barrier_semaphore()

    @pl.loop(1, ROWS)
    def _(j):
        pl.semaphore_signal(barrier, inc=1, device_id={"rows": row_peer(ROWS - j), "feat": feat},
                            device_id_type=MESH)
    feat_peers = [(dy, dl) for dy in (2, 1, 3) for dl in (1, 0)] + [(0, 1)]
    for dy, dl in feat_peers:
        pl.semaphore_signal(barrier, inc=1, device_id={"rows": row, "feat": feat_of(dy, dl)},
                            device_id_type=MESH)

    loads = [
        pltpu.make_async_copy(wi_h, wi, lsem.at[0]),
        pltpu.make_async_copy(wu_h, wu, lsem.at[1]),
        pltpu.make_async_copy(y_h, xv.at[pl.ds(0, K)], lsem.at[2]),
        pltpu.make_async_copy(x_h, xv.at[pl.ds(K, 2 * K)], lsem.at[3]),
        pltpu.make_async_copy(rat_h, rat, lsem.at[4]),
    ]
    for c in loads:
        c.start()
    idx_loc[...] = jnp.zeros_like(idx_loc)
    idx_loc[0:1, 0:K] = y_idx[...]
    idx_loc[1:3, 0:K] = x_idx[...]
    left = lax.broadcasted_iota(jnp.int32, (1, 2 * SH), 1) < SH
    for b in range(2):
        for p in range(ROWS // 2):
            pair = jnp.where(left, observed[b, 2 * p], observed[b, 2 * p + 1])
            mask[b:b + 1, p * 2 * SH:(p + 1) * 2 * SH] = pair.astype(f32)
    for c, table, blocks in ((loads[0], wi, wi3), (loads[1], wu, wu3)):
        c.wait()
        for i in range(blocks.shape[0]):
            blocks[i] = table[:, i * FBW:(i + 1) * FBW]
    pl.semaphore_wait(barrier, ROWS - 1 + len(feat_peers))

    @pl.loop(1, ROWS)
    def _(j):
        send(idx_loc, idx_all.at[row], IDX, rows=row_peer(ROWS - j))
    idx_all[row] = idx_loc[...]
    arrived(idx_all.at[pl.ds(0, ROWS - 1)], IDX)
    to_smem = pltpu.make_async_copy(idx_all, idx_s, lsem.at[5])
    to_smem.start()
    to_smem.wait()

    def pick(unit, dst, d):
        table = wi3 if unit == 0 else wu3
        for k in range(K):
            dst[k] = table[idx_s[d, unit, k]]

    def ask(unit, lo, hi, picks=True, sends=True):
        @pl.loop(lo, hi)
        def _(j):
            d = row_peer(ROWS - j)
            if picks:
                pick(unit, asend.at[unit, d], d)
            if sends:
                send(asend.at[unit, d], arecv.at[unit, row], A0 + unit, rows=d)

    def project(unit, dst):
        arrived(arecv.at[unit, pl.ds(0, ROWS - 1)], A0 + unit)
        for k in range(K):
            w = arecv[unit, :, k].astype(f32).reshape(RANK, FBW)
            wcat[:, k * FBW:(k + 1) * FBW] = w.astype(bf)
        half = TILE // 2
        for h in range(2):
            xt = jnp.concatenate(
                [xv[unit * K + k, h * half:(h + 1) * half] for k in range(K)], axis=1)
            p = dot(xt, wcat[...], NT)
            dst[h * 4:(h + 1) * 4] = p.astype(bf).reshape(4, SH, RANK)

    def quarter(y):
        return pl.ds(2 * y, 2)

    def y_scatter(src, dst, ch):
        for dy in (2, 1, 3):
            y = lax.rem(my + dy, NY)
            send(src.at[quarter(y)], dst.at[quarter(my)], ch, f=feat_of(dy, 0))
        dst[quarter(my)] = src[quarter(my)]

    def y_sum(dst, out, ch):
        arrived(dst.at[pl.ds(0, FEAT - 2)], ch)
        for l in range(2):
            total = dst[l].astype(f32)
            for y in range(1, NY):
                total = total + dst[2 * y + l].astype(f32)
            out[l] = total.astype(bf)

    def y_gather(dst, ch):
        for dy in (2, 1, 3):
            send(dst.at[quarter(my)], dst.at[quarter(my)], ch, f=feat_of(dy, 0))

    def y_full(dst, ch):
        arrived(dst.at[pl.ds(0, FEAT - 2)], ch)

    def s_send(i):
        if i not in DIRECT:
            y_scatter(apart.at[i], ayr.at[i], UY + i)
            return
        for dy, dl in feat_peers:
            f = feat_of(dy, dl)
            send(apart.at[i, f], ayr.at[i, feat], UY + i, f=f)
        ayr[i, feat] = apart[i, feat]

    def s_mid(i):
        if i not in DIRECT:
            y_sum(ayr.at[i], ays.at[i], UY + i)
            send(ays.at[i], alr.at[i], UL + i, f=feat_of(0, 1))
            return
        arrived(ayr.at[i, pl.ds(0, FEAT - 1)], UY + i)
        total = ayr[i, 0].astype(f32)
        for f in range(1, FEAT):
            total = total + ayr[i, f].astype(f32)
        full[i, feat] = total.astype(bf)
        for dy, dl in feat_peers:
            send(full.at[i, feat], full.at[i, feat], UG + i, f=feat_of(dy, dl))

    def s_out(i):
        if i not in DIRECT:
            arrived(alr.at[i], UL + i)
            full[i, quarter(my)] = (ays[i].astype(f32) + alr[i].astype(f32)).astype(bf)
            y_gather(full.at[i], UG + i)

    def s_wait(i):
        arrived(full.at[i, pl.ds(0, FEAT - (1 if i in DIRECT else 2))], UG + i)

    def residual(b):
        upt[...] = full[b].reshape(TILE, RANK).T

        @pl.loop(0, NX)
        def _(x):
            it = item_all[x].reshape(2 * TILE // 2, RANK)
            cols = pl.ds(pl.multiple_of(x * TILE, TILE), TILE)
            pred = dot(full[b].reshape(TILE, RANK), it, NT) * rank_scale
            r = mask[b:b + 1, cols] * (pred - rat[b * TILE:(b + 1) * TILE, cols].astype(f32))
            r = r.astype(bf)
            resid[:, cols] = r
            t = dot(upt[...], r, NN)
            if b == 0:
                tacc[:, cols] = t
            else:
                tacc[:, cols] += t
        for h in range(2):
            g = dot(resid[h * RANK:(h + 1) * RANK, :], item_all[...].reshape(ROWS * SH, RANK), NN)
            apart[2 + b, h * 4:(h + 1) * 4] = (g * grad_scale).astype(bf).reshape(4, SH, RANK)

    def block_grads(unit, src, out):
        gt = src[...].reshape(TILE, RANK).T
        for k in range(0, K, 2):
            two = jnp.concatenate([xv[unit * K + k], xv[unit * K + k + 1]], axis=1)
            o = dot(gt, two, NN)
            for i in range(2):
                s = o[:, i * FBW:(i + 1) * FBW].reshape(ROWS, RP, FBW)
                gsend[unit, :, k + i] = s.astype(bf)
        out[row] = gsend[unit, row]

    def give(unit, out, lo, hi):
        @pl.loop(lo, hi)
        def _(j):
            d = row_peer(ROWS - j)
            send(gsend.at[unit, d], out.at[row], G0 + unit, rows=d)

    def onehots():
        for unit in range(3):
            ids = idx_all[:, unit]
            blocks = ohi.shape[0] if unit == 0 else ohu.shape[1]
            lanes = lax.broadcasted_iota(jnp.int32, (ROWS, blocks), 1)
            rows = [jnp.where(ids[:, k:k + 1] == lanes, 1.0, 0.0) for k in range(K)]
            hot = jnp.concatenate(rows, axis=0).T.astype(bf)
            if unit == 0:
                ohi[...] = hot
            else:
                ohu[unit - 1] = hot

    def accumulate(returned, hot, out, first):
        for k in range(K):
            acc[k * RANK:(k + 1) * RANK] = returned[:, k].astype(f32).reshape(RANK, FBW)
        blocks = out.shape[0] // RP
        for r in range(0, RP, 2):
            two = jnp.concatenate(
                [acc[pl.ds(r + i, ROWS * K, stride=RP)].astype(bf) for i in range(2)], axis=1)
            o = dot(hot[...], two, NN)
            for i in range(2):
                v = o[:blocks, i * FBW:(i + 1) * FBW]
                at = pl.ds(r + i, blocks, stride=RP)
                if first:
                    out[at] = v
                else:
                    out[at] += v

    ask(0, 1, ROWS)
    ask(1, 1, 24)
    ask(1, 24, ROWS, sends=False)
    for unit in range(3):
        pick(unit, arecv.at[unit, row], row)
    for c in loads[2:]:
        c.wait()
    project(0, ipart)
    y_scatter(ipart, iyr, BY)
    ask(2, 1, ROWS, sends=False)
    y_sum(iyr, iys, BY)
    send(iys.at[1 - ml], ilr, BL, f=feat_of(0, 1))
    ask(1, 24, ROWS, picks=False)
    onehots()
    project(1, apart.at[0])
    s_send(0)
    arrived(ilr, BL)
    ishare[...] = (iys[ml].astype(f32) + ilr[...].astype(f32)).astype(bf)
    item_all[mx, mz, mc] = ishare[...]
    for dz in (2, 1, 3):
        send(ishare, item_all.at[mx, mz, mc], IZ, rows=row_of(0, dz, 0))
    ask(2, 1, 17, picks=False)
    s_mid(0)
    ask(2, 17, ROWS, picks=False)
    arrived(item_all.at[0, pl.ds(0, NZ - 1), 0], IZ)
    for dx in (2, 1, 3):
        send(item_all.at[mx, :, mc], item_all.at[mx, :, mc], IX, rows=row_of(dx, 0, 0))
    s_out(0)
    arrived(item_all.at[pl.ds(0, NX - 1), :, 0], IX)
    send(item_all.at[:, :, mc], item_all.at[:, :, mc], IC, rows=row_of(0, 0, 1))
    project(2, apart.at[1])
    s_send(1)
    arrived(item_all.at[:, :, 0], IC)
    s_wait(0)
    residual(0)
    s_send(2)
    s_mid(1)
    s_out(1)
    s_mid(2)
    s_out(2)
    s_wait(1)
    residual(1)
    s_send(3)
    s_wait(2)
    block_grads(1, full.at[2], gru.at[0])
    give(1, gru.at[0], 1, 16)

    for q in range(2 * NX):
        t = (tacc[:, q * RANK:(q + 1) * RANK] * grad_scale).T.astype(bf)
        for i in range(4):
            g = q * 4 + i
            ebuf[g // (2 * NZ), (g // 2) % NZ, g % 2] = t[i * SH:(i + 1) * SH]
    send(ebuf.at[:, :, 1 - mc], ecr, EC, rows=row_of(0, 0, 1))
    s_mid(3)
    give(1, gru.at[0], 16, ROWS)
    arrived(ecr, EC)

    @pl.loop(0, NX)
    def _(x):
        es[x] = (ebuf[x, :, mc].astype(f32) + ecr[x].astype(f32)).astype(bf)
    for dx in (2, 1, 3):
        send(es.at[lax.rem(mx + dx, NX)], exr.at[mx], EX, rows=row_of(dx, 0, 0))
    exr[mx] = es[mx]
    s_out(3)
    arrived(exr.at[pl.ds(0, NX - 1)], EX)
    for z in range(NZ):
        total = exr[0, z].astype(f32)
        for x in range(1, NX):
            total = total + exr[x, z].astype(f32)
        ez[z] = total.astype(bf)
    for dz in (2, 1, 3):
        send(ez.at[lax.rem(mz + dz, NZ)], ezr.at[mz], EZ, rows=row_of(0, dz, 0))
    ezr[mz] = ez[mz]
    s_wait(3)
    block_grads(2, full.at[3], gru.at[1])
    give(2, gru.at[1], 1, 12)
    arrived(ezr.at[pl.ds(0, NZ - 1)], EZ)
    total = ezr[0].astype(f32)
    for z in range(1, NZ):
        total = total + ezr[z].astype(f32)
    ifull[feat] = total.astype(bf)
    send(ifull.at[feat], ifull.at[feat], FL, f=feat_of(0, 1))
    give(2, gru.at[1], 12, ROWS)
    arrived(ifull.at[0], FL)
    y_gather(ifull, FY)
    y_full(ifull, FY)
    block_grads(0, ifull, gri)
    give(0, gri, 1, ROWS)

    arrived(gru.at[0, pl.ds(0, ROWS - 1)], G0 + 1)
    accumulate(gru.at[0], ohu.at[0], out_u, True)
    arrived(gru.at[1, pl.ds(0, ROWS - 1)], G0 + 2)
    accumulate(gru.at[1], ohu.at[1], out_u, False)
    arrived(gri.at[pl.ds(0, ROWS - 1)], G0)
    accumulate(gri, ohi, out_i, True)
    for c in unsent:
        c.wait_send()


def on_device(x_vals, x_blocks, y_vals, y_blocks, user_weights, item_weights, observed, ratings):
    bf, f32 = jnp.bfloat16, jnp.float32
    V = pltpu.VMEM
    n_u, n_i = user_weights.shape[1] // FBW, item_weights.shape[1] // FBW
    pad_u, pad_i = -(-n_u // FBW) * FBW, -(-n_i // FBW) * FBW
    slab = (SH, RANK)
    items = (NX, NZ, 2, SH, RANK)
    out_u, out_i = pl.pallas_call(
        kernel,
        out_shape=(jax.ShapeDtypeStruct((n_u * RP, FBW), f32),
                   jax.ShapeDtypeStruct((n_i * RP, FBW), f32)),
        in_specs=[pl.BlockSpec(memory_space=pltpu.VMEM)] * 2
        + [pl.BlockSpec(memory_space=pltpu.SMEM)]
        + [pl.BlockSpec(memory_space=pl.ANY)] * 5,
        out_specs=[pl.BlockSpec(memory_space=pltpu.VMEM)] * 2,
        scratch_shapes=[
            V((2, ROWS, K, RP, FBW), bf), V((ROWS, K, RP, FBW), bf), V((ROWS, 4, FBW), jnp.int32),
            V((2, pad_u, ROWS * K), bf), V((pad_i, ROWS * K), bf), V((K * RANK, FBW), f32),
            V(user_weights.shape, bf), V(item_weights.shape, bf),
            V((n_u, RP, FBW), bf), V((n_i, RP, FBW), bf),
            V((3 * K, TILE, FBW), bf), V((2 * TILE, ROWS * SH), bf), V((2, ROWS * SH), f32),
            V((4, FBW), jnp.int32), pltpu.SMEM((ROWS, 4, FBW), jnp.int32),
            V((3, ROWS, K, RP, FBW), bf), V((3, ROWS, K, RP, FBW), bf), V((RANK, K * FBW), bf),
            V((FEAT, *slab), bf), V((FEAT, *slab), bf), V((2, *slab), bf), V(slab, bf), V(slab, bf),
            V((4, FEAT, *slab), bf), V((4, FEAT, *slab), bf), V((4, 2, *slab), bf),
            V((4, 2, *slab), bf), V((4, FEAT, *slab), bf),
            V(items, bf), V((TILE, ROWS * SH), bf), V((RANK, ROWS * SH), f32),
            V(items, bf), V((NX, NZ, *slab), bf), V((NX, NZ, *slab), bf), V((NX, NZ, *slab), bf),
            V((NZ, *slab), bf), V((NZ, *slab), bf), V((FEAT, *slab), bf),
            V((3, ROWS, K, RP, FBW), bf), V((RANK, TILE), bf), pltpu.SemaphoreType.DMA((6,)),
            pltpu.SemaphoreType.DMA((NCH,)), pltpu.SemaphoreType.DMA((NCH,)),
        ],
        compiler_params=pltpu.CompilerParams(collective_id=0, has_side_effects=True),
        name="step",
    )(x_blocks.reshape(2, K), y_blocks.reshape(1, K), observed, user_weights, item_weights,
      x_vals.reshape(2 * K, TILE, FBW), y_vals.reshape(K, TILE, FBW),
      ratings.reshape(2 * TILE, ROWS * SH))
    return (out_u.reshape(n_u, RP, FBW).swapaxes(0, 1).reshape(user_weights.shape),
            out_i.reshape(n_i, RP, FBW).swapaxes(0, 1).reshape(item_weights.shape))


def solution(mesh):
    return jax.shard_map(
        on_device,
        mesh=mesh,
        in_specs=(
            P("rows", "feat", None, None, None),
            P("rows", "feat", None),
            P("rows", "feat", None, None, None),
            P("rows", "feat", None),
            P("rows", "feat"),
            P("rows", "feat"),
            P("rows", None),
            P("rows", "feat", None),
        ),
        out_specs=(P("rows", "feat"), P("rows", "feat")),
        check_vma=False,
    )
```

```python
import math

import jax
import jax.numpy as jnp
from jax import lax
from jax.experimental import pallas as pl
from jax.experimental.pallas import tpu as pltpu
from jax.sharding import PartitionSpec as P

TILE = 512
FBW = 128
RANK = 256
ROWS = 32
FEAT = 8
NX = 4
NZ = 4
K = 8
SH = TILE // FEAT
NY = FEAT // 2
RP = RANK // ROWS
MESH = pl.DeviceIdType.MESH
DIRECT = (1, 2)

IDX, A0, BY, BL, IZ, IX, IC, EX, EZ, FL, FY, G0, UY, UL, UG, EC, NCH = (
    0, 1, 4, 5, 6, 7, 8, 9, 10, 11, 12, 13, 16, 20, 24, 28, 32)

NT = (((1,), (1,)), ((), ()))
NN = (((1,), (0,)), ((), ()))


def dot(a, b, dims):
    return lax.dot_general(a, b, dims, preferred_element_type=jnp.float32)


def kernel(x_idx, y_idx, observed, wu_h, wi_h, x_h, y_h, rat_h, out_u, out_i,
           gru, gri, idx_all, ohu, ohi, acc, wu, wi, wu3, wi3, xv, rat, mask, idx_loc, idx_s, asend, arecv, wcat, ipart,
           iyr, iys, ilr, ishare, apart, ayr, ays, alr, full, item_all, resid, tacc,
           ebuf, ecr, es, exr, ez, ezr, ifull, gsend, upt, lsem, ssem, rsem):
    row = lax.axis_index("rows")
    feat = lax.axis_index("feat")
    mx = row // (2 * NZ)
    mz = lax.rem(row // 2, NZ)
    mc = lax.rem(row, 2)
    my = feat // 2
    ml = lax.rem(feat, 2)
    bf, f32 = jnp.bfloat16, jnp.float32
    rank_scale = 1.0 / math.sqrt(RANK)
    grad_scale = 1.0 / (TILE * math.sqrt(RANK))

    def row_of(dx, dz, dc):
        return (lax.rem(mx + dx, NX) * (2 * NZ) + lax.rem(mz + dz, NZ) * 2
                + lax.rem(mc + dc, 2))

    def row_peer(j):
        return row_of(lax.rem(j // NZ, NX), lax.rem(j, NZ), j // (NX * NZ))

    def feat_of(dy, dl):
        return lax.rem(my + dy, NY) * 2 + lax.rem(ml + dl, 2)

    def copy(src, dst, ch, rows=None, f=None):
        return pltpu.make_async_remote_copy(
            src_ref=src, dst_ref=dst, send_sem=ssem.at[ch], recv_sem=rsem.at[ch],
            device_id={"rows": row if rows is None else rows, "feat": feat if f is None else f},
            device_id_type=MESH)

    unsent = []

    def send(src, dst, ch, rows=None, f=None):
        copy(src, dst, ch, rows, f).start()

    def arrived(ref, ch):
        c = copy(ref, ref, ch, rows=row_of(0, 0, 1))
        c.wait_recv()
        unsent.append(c)

    barrier = pltpu.get_barrier_semaphore()

    @pl.loop(1, ROWS)
    def _(j):
        pl.semaphore_signal(barrier, inc=1, device_id={"rows": row_peer(ROWS - j), "feat": feat},
                            device_id_type=MESH)
    feat_peers = [(dy, dl) for dy in (2, 1, 3) for dl in (1, 0)] + [(0, 1)]
    for dy, dl in feat_peers:
        pl.semaphore_signal(barrier, inc=1, device_id={"rows": row, "feat": feat_of(dy, dl)},
                            device_id_type=MESH)

    loads = [
        pltpu.make_async_copy(wi_h, wi, lsem.at[0]),
        pltpu.make_async_copy(wu_h, wu, lsem.at[1]),
        pltpu.make_async_copy(y_h, xv.at[pl.ds(0, K)], lsem.at[2]),
        pltpu.make_async_copy(x_h, xv.at[pl.ds(K, 2 * K)], lsem.at[3]),
        pltpu.make_async_copy(rat_h, rat, lsem.at[4]),
    ]
    for c in loads:
        c.start()
    idx_loc[...] = jnp.zeros_like(idx_loc)
    idx_loc[0:1, 0:K] = y_idx[...]
    idx_loc[1:3, 0:K] = x_idx[...]
    left = lax.broadcasted_iota(jnp.int32, (1, 2 * SH), 1) < SH
    for b in range(2):
        for p in range(ROWS // 2):
            pair = jnp.where(left, observed[b, 2 * p], observed[b, 2 * p + 1])
            mask[b:b + 1, p * 2 * SH:(p + 1) * 2 * SH] = pair.astype(f32)
    for c, table, blocks in ((loads[0], wi, wi3), (loads[1], wu, wu3)):
        c.wait()
        for i in range(blocks.shape[0]):
            blocks[i] = table[:, i * FBW:(i + 1) * FBW]
    pl.semaphore_wait(barrier, ROWS - 1 + len(feat_peers))

    @pl.loop(1, ROWS)
    def _(j):
        send(idx_loc, idx_all.at[row], IDX, rows=row_peer(ROWS - j))
    idx_all[row] = idx_loc[...]
    arrived(idx_all.at[pl.ds(0, ROWS - 1)], IDX)
    to_smem = pltpu.make_async_copy(idx_all, idx_s, lsem.at[5])
    to_smem.start()
    to_smem.wait()

    def pick(unit, dst, d):
        table = wi3 if unit == 0 else wu3
        for k in range(K):
            dst[k] = table[idx_s[d, unit, k]]

    def ask(unit, lo, hi, picks=True, sends=True):
        @pl.loop(lo, hi)
        def _(j):
            d = row_peer(ROWS - j)
            if picks:
                pick(unit, asend.at[unit, d], d)
            if sends:
                send(asend.at[unit, d], arecv.at[unit, row], A0 + unit, rows=d)

    def project(unit, dst):
        arrived(arecv.at[unit, pl.ds(0, ROWS - 1)], A0 + unit)
        for k in range(K):
            w = arecv[unit, :, k].astype(f32).reshape(RANK, FBW)
            wcat[:, k * FBW:(k + 1) * FBW] = w.astype(bf)
        half = TILE // 2
        for h in range(2):
            xt = jnp.concatenate(
                [xv[unit * K + k, h * half:(h + 1) * half] for k in range(K)], axis=1)
            p = dot(xt, wcat[...], NT)
            dst[h * 4:(h + 1) * 4] = p.astype(bf).reshape(4, SH, RANK)

    def quarter(y):
        return pl.ds(2 * y, 2)

    def y_scatter(src, dst, ch):
        for dy in (2, 1, 3):
            y = lax.rem(my + dy, NY)
            send(src.at[quarter(y)], dst.at[quarter(my)], ch, f=feat_of(dy, 0))
        dst[quarter(my)] = src[quarter(my)]

    def y_sum(dst, out, ch):
        arrived(dst.at[pl.ds(0, FEAT - 2)], ch)
        for l in range(2):
            total = dst[l].astype(f32)
            for y in range(1, NY):
                total = total + dst[2 * y + l].astype(f32)
            out[l] = total.astype(bf)

    def y_gather(dst, ch):
        for dy in (2, 1, 3):
            send(dst.at[quarter(my)], dst.at[quarter(my)], ch, f=feat_of(dy, 0))

    def y_full(dst, ch):
        arrived(dst.at[pl.ds(0, FEAT - 2)], ch)

    def s_send(i):
        if i not in DIRECT:
            y_scatter(apart.at[i], ayr.at[i], UY + i)
            return
        for dy, dl in feat_peers:
            f = feat_of(dy, dl)
            send(apart.at[i, f], ayr.at[i, feat], UY + i, f=f)
        ayr[i, feat] = apart[i, feat]

    def s_mid(i):
        if i not in DIRECT:
            y_sum(ayr.at[i], ays.at[i], UY + i)
            send(ays.at[i], alr.at[i], UL + i, f=feat_of(0, 1))
            return
        arrived(ayr.at[i, pl.ds(0, FEAT - 1)], UY + i)
        total = ayr[i, 0].astype(f32)
        for f in range(1, FEAT):
            total = total + ayr[i, f].astype(f32)
        full[i, feat] = total.astype(bf)
        for dy, dl in feat_peers:
            send(full.at[i, feat], full.at[i, feat], UG + i, f=feat_of(dy, dl))

    def s_out(i):
        if i not in DIRECT:
            arrived(alr.at[i], UL + i)
            full[i, quarter(my)] = (ays[i].astype(f32) + alr[i].astype(f32)).astype(bf)
            y_gather(full.at[i], UG + i)

    def s_wait(i):
        arrived(full.at[i, pl.ds(0, FEAT - (1 if i in DIRECT else 2))], UG + i)

    def residual(b):
        upt[...] = full[b].reshape(TILE, RANK).T

        @pl.loop(0, NX)
        def _(x):
            it = item_all[x].reshape(2 * TILE // 2, RANK)
            cols = pl.ds(pl.multiple_of(x * TILE, TILE), TILE)
            pred = dot(full[b].reshape(TILE, RANK), it, NT) * rank_scale
            r = mask[b:b + 1, cols] * (pred - rat[b * TILE:(b + 1) * TILE, cols].astype(f32))
            r = r.astype(bf)
            resid[:, cols] = r
            t = dot(upt[...], r, NN)
            if b == 0:
                tacc[:, cols] = t
            else:
                tacc[:, cols] += t
        for h in range(2):
            g = dot(resid[h * RANK:(h + 1) * RANK, :], item_all[...].reshape(ROWS * SH, RANK), NN)
            apart[2 + b, h * 4:(h + 1) * 4] = (g * grad_scale).astype(bf).reshape(4, SH, RANK)

    def block_grads(unit, src, out):
        gt = src[...].reshape(TILE, RANK).T
        for k in range(0, K, 2):
            two = jnp.concatenate([xv[unit * K + k], xv[unit * K + k + 1]], axis=1)
            o = dot(gt, two, NN)
            for i in range(2):
                s = o[:, i * FBW:(i + 1) * FBW].reshape(ROWS, RP, FBW)
                gsend[unit, :, k + i] = s.astype(bf)
        out[row] = gsend[unit, row]

    def give(unit, out, lo, hi):
        @pl.loop(lo, hi)
        def _(j):
            d = row_peer(ROWS - j)
            send(gsend.at[unit, d], out.at[row], G0 + unit, rows=d)

    def onehots():
        for unit in range(3):
            ids = idx_all[:, unit]
            blocks = ohi.shape[0] if unit == 0 else ohu.shape[1]
            lanes = lax.broadcasted_iota(jnp.int32, (ROWS, blocks), 1)
            rows = [jnp.where(ids[:, k:k + 1] == lanes, 1.0, 0.0) for k in range(K)]
            hot = jnp.concatenate(rows, axis=0).T.astype(bf)
            if unit == 0:
                ohi[...] = hot
            else:
                ohu[unit - 1] = hot

    def accumulate(returned, hot, out, first):
        for k in range(K):
            acc[k * RANK:(k + 1) * RANK] = returned[:, k].astype(f32).reshape(RANK, FBW)
        blocks = out.shape[0] // RP
        for r in range(0, RP, 2):
            two = jnp.concatenate(
                [acc[pl.ds(r + i, ROWS * K, stride=RP)].astype(bf) for i in range(2)], axis=1)
            o = dot(hot[...], two, NN)
            for i in range(2):
                v = o[:blocks, i * FBW:(i + 1) * FBW]
                at = pl.ds(r + i, blocks, stride=RP)
                if first:
                    out[at] = v
                else:
                    out[at] += v

    ask(0, 1, ROWS)
    ask(1, 1, 24)
    ask(1, 24, ROWS, sends=False)
    for unit in range(3):
        pick(unit, arecv.at[unit, row], row)
    for c in loads[2:]:
        c.wait()
    project(0, ipart)
    y_scatter(ipart, iyr, BY)
    ask(2, 1, ROWS, sends=False)
    y_sum(iyr, iys, BY)
    send(iys.at[1 - ml], ilr, BL, f=feat_of(0, 1))
    ask(1, 24, ROWS, picks=False)
    onehots()
    project(1, apart.at[0])
    s_send(0)
    arrived(ilr, BL)
    ishare[...] = (iys[ml].astype(f32) + ilr[...].astype(f32)).astype(bf)
    item_all[mx, mz, mc] = ishare[...]
    for dz in (2, 1, 3):
        send(ishare, item_all.at[mx, mz, mc], IZ, rows=row_of(0, dz, 0))
    ask(2, 1, 17, picks=False)
    s_mid(0)
    ask(2, 17, ROWS, picks=False)
    arrived(item_all.at[0, pl.ds(0, NZ - 1), 0], IZ)
    for dx in (2, 1, 3):
        send(item_all.at[mx, :, mc], item_all.at[mx, :, mc], IX, rows=row_of(dx, 0, 0))
    s_out(0)
    arrived(item_all.at[pl.ds(0, NX - 1), :, 0], IX)
    send(item_all.at[:, :, mc], item_all.at[:, :, mc], IC, rows=row_of(0, 0, 1))
    project(2, apart.at[1])
    s_send(1)
    arrived(item_all.at[:, :, 0], IC)
    s_wait(0)
    residual(0)
    s_send(2)
    s_mid(1)
    s_out(1)
    s_mid(2)
    s_out(2)
    s_wait(1)
    residual(1)
    s_send(3)
    s_wait(2)
    block_grads(1, full.at[2], gru.at[0])
    give(1, gru.at[0], 1, 16)

    for dx in (2, 1, 3, 0):
        x = lax.rem(mx + dx, NX)
        for h in range(2):
            cols = pl.ds(pl.multiple_of(x * TILE + h * RANK, RANK), RANK)
            t = (tacc[:, cols] * grad_scale).T.astype(bf)
            for i in range(4):
                ebuf[x, h * 2 + i // 2, i % 2] = t[i * SH:(i + 1) * SH]
        send(ebuf.at[x, :, 1 - mc], ecr.at[x], EC + dx, rows=row_of(0, 0, 1))
    s_mid(3)
    give(1, gru.at[0], 16, ROWS)
    for dx in (2, 1, 3, 0):
        x = lax.rem(mx + dx, NX)
        arrived(ecr.at[0], EC + dx)
        both = (ebuf[x, :, mc].astype(f32) + ecr[x].astype(f32)).astype(bf)
        if dx:
            es[x] = both
            send(es.at[x], exr.at[mx], EX, rows=row_of(dx, 0, 0))
        else:
            exr[mx] = both
    s_out(3)
    arrived(exr.at[pl.ds(0, NX - 1)], EX)
    for z in range(NZ):
        total = exr[0, z].astype(f32)
        for x in range(1, NX):
            total = total + exr[x, z].astype(f32)
        ez[z] = total.astype(bf)
    for dz in (2, 1, 3):
        send(ez.at[lax.rem(mz + dz, NZ)], ezr.at[mz], EZ, rows=row_of(0, dz, 0))
    ezr[mz] = ez[mz]
    s_wait(3)
    block_grads(2, full.at[3], gru.at[1])
    give(2, gru.at[1], 1, 12)
    arrived(ezr.at[pl.ds(0, NZ - 1)], EZ)
    total = ezr[0].astype(f32)
    for z in range(1, NZ):
        total = total + ezr[z].astype(f32)
    ifull[feat] = total.astype(bf)
    send(ifull.at[feat], ifull.at[feat], FL, f=feat_of(0, 1))
    give(2, gru.at[1], 12, ROWS)
    arrived(ifull.at[0], FL)
    y_gather(ifull, FY)
    y_full(ifull, FY)
    block_grads(0, ifull, gri)
    give(0, gri, 1, ROWS)

    arrived(gru.at[0, pl.ds(0, ROWS - 1)], G0 + 1)
    accumulate(gru.at[0], ohu.at[0], out_u, True)
    arrived(gru.at[1, pl.ds(0, ROWS - 1)], G0 + 2)
    accumulate(gru.at[1], ohu.at[1], out_u, False)
    arrived(gri.at[pl.ds(0, ROWS - 1)], G0)
    accumulate(gri, ohi, out_i, True)
    for c in unsent:
        c.wait_send()


def on_device(x_vals, x_blocks, y_vals, y_blocks, user_weights, item_weights, observed, ratings):
    bf, f32 = jnp.bfloat16, jnp.float32
    V = pltpu.VMEM
    n_u, n_i = user_weights.shape[1] // FBW, item_weights.shape[1] // FBW
    pad_u, pad_i = -(-n_u // FBW) * FBW, -(-n_i // FBW) * FBW
    slab = (SH, RANK)
    items = (NX, NZ, 2, SH, RANK)
    out_u, out_i = pl.pallas_call(
        kernel,
        out_shape=(jax.ShapeDtypeStruct((n_u * RP, FBW), f32),
                   jax.ShapeDtypeStruct((n_i * RP, FBW), f32)),
        in_specs=[pl.BlockSpec(memory_space=pltpu.VMEM)] * 2
        + [pl.BlockSpec(memory_space=pltpu.SMEM)]
        + [pl.BlockSpec(memory_space=pl.ANY)] * 5,
        out_specs=[pl.BlockSpec(memory_space=pltpu.VMEM)] * 2,
        scratch_shapes=[
            V((2, ROWS, K, RP, FBW), bf), V((ROWS, K, RP, FBW), bf), V((ROWS, 4, FBW), jnp.int32),
            V((2, pad_u, ROWS * K), bf), V((pad_i, ROWS * K), bf), V((K * RANK, FBW), f32),
            V(user_weights.shape, bf), V(item_weights.shape, bf),
            V((n_u, RP, FBW), bf), V((n_i, RP, FBW), bf),
            V((3 * K, TILE, FBW), bf), V((2 * TILE, ROWS * SH), bf), V((2, ROWS * SH), f32),
            V((4, FBW), jnp.int32), pltpu.SMEM((ROWS, 4, FBW), jnp.int32),
            V((3, ROWS, K, RP, FBW), bf), V((3, ROWS, K, RP, FBW), bf), V((RANK, K * FBW), bf),
            V((FEAT, *slab), bf), V((FEAT, *slab), bf), V((2, *slab), bf), V(slab, bf), V(slab, bf),
            V((4, FEAT, *slab), bf), V((4, FEAT, *slab), bf), V((4, 2, *slab), bf),
            V((4, 2, *slab), bf), V((4, FEAT, *slab), bf),
            V(items, bf), V((TILE, ROWS * SH), bf), V((RANK, ROWS * SH), f32),
            V(items, bf), V((NX, NZ, *slab), bf), V((NX, NZ, *slab), bf), V((NX, NZ, *slab), bf),
            V((NZ, *slab), bf), V((NZ, *slab), bf), V((FEAT, *slab), bf),
            V((3, ROWS, K, RP, FBW), bf), V((RANK, TILE), bf), pltpu.SemaphoreType.DMA((6,)),
            pltpu.SemaphoreType.DMA((NCH,)), pltpu.SemaphoreType.DMA((NCH,)),
        ],
        compiler_params=pltpu.CompilerParams(collective_id=0, has_side_effects=True),
        name="step",
    )(x_blocks.reshape(2, K), y_blocks.reshape(1, K), observed, user_weights, item_weights,
      x_vals.reshape(2 * K, TILE, FBW), y_vals.reshape(K, TILE, FBW),
      ratings.reshape(2 * TILE, ROWS * SH))
    return (out_u.reshape(n_u, RP, FBW).swapaxes(0, 1).reshape(user_weights.shape),
            out_i.reshape(n_i, RP, FBW).swapaxes(0, 1).reshape(item_weights.shape))


def solution(mesh):
    return jax.shard_map(
        on_device,
        mesh=mesh,
        in_specs=(
            P("rows", "feat", None, None, None),
            P("rows", "feat", None),
            P("rows", "feat", None, None, None),
            P("rows", "feat", None),
            P("rows", "feat"),
            P("rows", "feat"),
            P("rows", None),
            P("rows", "feat", None),
        ),
        out_specs=(P("rows", "feat"), P("rows", "feat")),
        check_vma=False,
    )
```
